32 devices in a mesh: fsdp: 4 (over y, core), ctx: 2 (over x), tp: 4 (over z).
Axes of the slice: x: 2, y: 2, z: 4, core: 2. Of those that a mesh axis runs over, the one named last changes fastest.
Arguments:
- block_input: bfloat16 [4096, 768], P(('fsdp', 'ctx', 'tp')), may hold values from -6 to 6
- cotangent: bfloat16 [4096, 768], P(('fsdp', 'ctx', 'tp'))
- norm1_gain: bfloat16 [768], replicated, may hold values from 0.25 to 1.75
- norm1_bias: bfloat16 [768], replicated, may hold values from -1.796875 to 1.796875
- norm2_gain: bfloat16 [768], replicated, may hold values from 0.25 to 1.75
- norm2_bias: bfloat16 [768], replicated, may hold values from -1.796875 to 1.796875
- qkv_weight: bfloat16 [3, 768, 768], P(None, ('fsdp', 'ctx'), 'tp')
- qkv_bias: bfloat16 [3, 768], P(None, 'tp'), may hold values from -3 to 3
- out_weight: bfloat16 [768, 768], P('tp', ('fsdp', 'ctx')), may hold values from -0.875 to 0.875
- out_bias: bfloat16 [768], replicated, may hold values from -1.796875 to 1.796875
- up_weight: bfloat16 [768, 3072], P(('fsdp', 'ctx'), 'tp'), may hold values from -0.21875 to 0.21875
- up_bias: bfloat16 [3072], P('tp'), may hold values from -3 to 3
- down_weight: bfloat16 [3072, 768], P('tp', ('fsdp', 'ctx')), may hold values from -0.109375 to 0.109375
- down_bias: bfloat16 [768], replicated, may hold values from -1.796875 to 1.796875
- doc_ids: int32 [4096], P(('fsdp', 'ctx')), may hold values from 0 to 7, as said below
- doc_start: int32 [4096], P(('fsdp', 'ctx')), may hold values from 0 to 1023, as said below
Outputs:
- block_output: bfloat16 [4096, 768], P(('fsdp', 'ctx', 'tp'))
- grad_input: bfloat16 [4096, 768], P(('fsdp', 'ctx', 'tp'))
- grad_qkv_weight: float32 [3, 768, 768], P(None, ('fsdp', 'ctx'), 'tp')
- grad_qkv_bias: float32 [3, 768], P(None, 'tp')
- grad_out_weight: float32 [768, 768], P('tp', ('fsdp', 'ctx'))
- grad_out_bias: float32 [768], replicated
- grad_up_weight: float32 [768, 3072], P(('fsdp', 'ctx'), 'tp')
- grad_up_bias: float32 [3072], P('tp')
- grad_down_weight: float32 [3072, 768], P('tp', ('fsdp', 'ctx'))
- grad_down_bias: float32 [768], replicated
- grad_norm1_gain: float32 [768], replicated
- grad_norm1_bias: float32 [768], replicated
- grad_norm2_gain: float32 [768], replicated
- grad_norm2_bias: float32 [768], replicated
The draws below stay inside these ranges and needn't reach their ends.
Inputs may be any that keep to these rules, and one draw needn't show every extreme that they name: `doc_ids`: numbers the documents of each sequence of 1024 tokens from 0 at the sequence's first token; within a sequence it never falls and rises by one at the first token of each document; a sequence holds at most 8 documents. `doc_start`: the position within its sequence of the first token of the token's document: 0 at each sequence's first token, a token's own position where its document begins, equal for all tokens of one document.
All inputs are finite; a program needn't handle non-finite values.
Results may differ from the reference program's by a relative error of at most 0.009.
Values may be sent and summed in bfloat16 or wider, within the bound.
A program may use at most 128 MiB of HBM per device.

```python
import jax
import jax.numpy as jnp
from jax import lax

D = 768
FF = 3072
HEADS = 12
HD = 64
ROT = 16
LEN = 1024
TOKENS = 4096


def document_layout(key):
    base_key = jax.random.fold_in(key, 4242)
    seq_count = TOKENS // LEN
    count_key = jax.random.fold_in(base_key, 1)
    order_key = jax.random.fold_in(base_key, 2)
    doc_counts = jax.random.randint(count_key, (seq_count,), 1, 9)
    first_flag = (jnp.arange(seq_count, dtype=jnp.int32) == 0).astype(jnp.int32)
    doc_counts = jnp.where(first_flag == 1, 8, doc_counts)
    extra = doc_counts - 1 - first_flag
    order_keys = jax.random.split(order_key, seq_count)
    ranks = jax.vmap(lambda one_key: jax.random.permutation(one_key, LEN - 2))(order_keys)
    inner = ranks < extra[:, None]
    head_col = jnp.ones((seq_count, 1), dtype=bool)
    tail_col = (first_flag == 1)[:, None]
    begins = jnp.concatenate([head_col, inner, tail_col], axis=1)
    column = jnp.arange(LEN, dtype=jnp.int32)[None, :]
    numbers = jnp.cumsum(begins.astype(jnp.int32), axis=1) - 1
    starts = lax.cummax(jnp.where(begins, column, 0), axis=1)
    return (numbers.reshape(TOKENS).astype(jnp.int32), starts.reshape(TOKENS).astype(jnp.int32))


def draw_doc_ids(key, part):
    return document_layout(key)[0]


def draw_doc_start(key, part):
    return document_layout(key)[1]


def draw_cotangent(key, part):
    row_scale = 0.5 + jnp.arange(TOKENS, dtype=jnp.float32)[:, None] / TOKENS
    sample = jax.random.normal(key, (TOKENS, D), jnp.float32)
    return (sample * row_scale).astype(jnp.bfloat16)


def draw_qkv_weight(key, part):
    sample = jax.random.normal(key, (3, D, D), jnp.float32) * D ** (-0.5)
    return sample.astype(jnp.bfloat16)


def levels(own_key, dims, cuts, least, largest):
    factor_of, own = 1.0, jax.random.fold_in(own_key, 6)
    for position, shards_of in cuts:
        steps = jnp.exp(jax.random.uniform(jax.random.fold_in(own, position), (shards_of,), jnp.float32, least / len(cuts), largest / len(cuts)))
        factor_of = factor_of * jnp.repeat(steps, dims[position] // shards_of).reshape([-1 if axis == position else 1 for axis in range(len(dims))])
    return factor_of


def centred(key, dims, spread, reach, shards=(), kind=jnp.bfloat16):
    factor_of = levels(key, dims, shards, -0.22, 0.18) if shards else 1.0
    values = jax.random.normal(key, dims, jnp.float32) * spread * factor_of
    return jnp.minimum(jnp.maximum(values, -reach), reach).astype(kind)


def setup_inputs(seed: int = 0) -> dict:
    streams_of = jax.random.split(jax.random.key(seed), 17)
    return {
        "block_input": centred(streams_of[0], (TOKENS, D), 1.0, 6.0, ((0, 32),)),
        "cotangent": draw_cotangent(jax.random.fold_in(streams_of[16], 71), 0),
        "norm1_gain": jnp.clip(1.0 + 0.15 * jax.random.normal(streams_of[2], (D,), jnp.float32), 0.25, 1.75).astype(jnp.bfloat16),
        "norm1_bias": centred(streams_of[3], (D,), 0.3, 1.796875),
        "norm2_gain": jnp.clip(1.0 + 0.15 * jax.random.normal(streams_of[4], (D,), jnp.float32), 0.25, 1.75).astype(jnp.bfloat16),
        "norm2_bias": centred(streams_of[5], (D,), 0.3, 1.796875),
        "qkv_weight": draw_qkv_weight(jax.random.fold_in(streams_of[16], 71), 0),
        "qkv_bias": centred(streams_of[7], (3, D), 0.5, 3.0, ((1, 4),)),
        "out_weight": centred(streams_of[8], (D, D), (D // 16) ** -0.5, 0.875, ((0, 4), (1, 8))),
        "out_bias": centred(streams_of[9], (D,), 0.3, 1.796875),
        "up_weight": centred(streams_of[10], (D, FF), D ** -0.5, 0.21875, ((0, 8), (1, 4))),
        "up_bias": centred(streams_of[11], (FF,), 0.5, 3.0, ((0, 4),)),
        "down_weight": centred(streams_of[12], (FF, D), FF ** -0.5, 0.109375, ((0, 4), (1, 8))),
        "down_bias": centred(streams_of[13], (D,), 0.3, 1.796875),
        "doc_ids": draw_doc_ids(jax.random.fold_in(streams_of[16], 71), 0),
        "doc_start": draw_doc_start(jax.random.fold_in(streams_of[16], 71), 0),
    }


EPS = 1e-05

def gelu_parts(pre_act):
    cumulative = 0.5 * (1.0 + jax.scipy.special.erf(pre_act * 0.7071067811865476))
    density = jnp.exp(-0.5 * pre_act * pre_act) * 0.3989422804014327
    return (pre_act * cumulative, cumulative + pre_act * density)

def angle_tables(offsets):
    half_rot = ROT // 2
    frequency = 10000.0 ** (-(2.0 * jnp.arange(half_rot, dtype=jnp.float32)) / ROT)
    angles = offsets.astype(jnp.float32)[:, None] * frequency[None, :]
    angles = jnp.concatenate([angles, angles], axis=1)
    return (jnp.cos(angles), jnp.sin(angles))

def rotate(tensor, cosine, sine_table):
    half_rot = ROT // 2
    turned = jnp.concatenate([-tensor[..., half_rot:ROT], tensor[..., :half_rot]], axis=-1)
    leading = tensor[..., :ROT] * cosine[:, None, :] + turned * sine_table[:, None, :]
    return jnp.concatenate([leading, tensor[..., ROT:]], axis=-1)

def normalize(rows_in):
    centered = rows_in - lax.optimization_barrier(jnp.mean(rows_in, axis=1, keepdims=True))
    inv_std = lax.rsqrt(lax.optimization_barrier(jnp.mean(centered * centered, axis=1, keepdims=True)) + EPS)
    return (centered * inv_std, inv_std)

def attention_probs(queries, keys_all, query_pos, query_doc, key_doc):
    score_scale = HD ** (-0.5)
    scores = jnp.einsum('qhd,khd->hqk', queries, keys_all) * score_scale
    key_pos = jnp.arange(keys_all.shape[0], dtype=jnp.int32)
    allowed = (query_doc[:, None] == key_doc[None, :]) & (key_pos[None, :] <= query_pos[:, None])
    masked = jnp.where(allowed[None], scores, -1e+30)
    row_peak = lax.optimization_barrier(jnp.max(masked, axis=2, keepdims=True))
    exponent = jnp.where(allowed[None], jnp.exp(masked - row_peak), 0.0)
    return exponent / lax.optimization_barrier(jnp.sum(exponent, axis=2, keepdims=True))

def reference(block_input, cotangent, norm1_gain, norm1_bias, norm2_gain, norm2_bias, qkv_weight, qkv_bias, out_weight, out_bias, up_weight, up_bias, down_weight, down_bias, doc_ids, doc_start):
    seq_count = TOKENS // LEN
    score_scale = HD ** (-0.5)
    gain_one = norm1_gain.astype(jnp.float32)
    bias_one = norm1_bias.astype(jnp.float32)
    gain_two = norm2_gain.astype(jnp.float32)
    bias_two = norm2_bias.astype(jnp.float32)

    def one_sequence(totals, pieces):
        seq_in, seq_cot, seq_doc, seq_start = pieces
        seq_float = seq_in.astype(jnp.float32)
        normed, inv_std = normalize(seq_float)
        first_in = (normed * gain_one + bias_one).astype(jnp.bfloat16)
        second_in = (normed * gain_two + bias_two).astype(jnp.bfloat16)
        projected = jnp.stack([jnp.dot(first_in, qkv_weight[part_idx], preferred_element_type=jnp.float32) for part_idx in range(3)])
        projected = projected + qkv_bias.astype(jnp.float32)[:, None, :]
        positions = jnp.arange(LEN, dtype=jnp.int32)
        cosine, sine_table = angle_tables(positions - seq_start)
        queries = rotate(projected[0].reshape(LEN, HEADS, HD), cosine, sine_table).astype(jnp.bfloat16)
        keys_all = rotate(projected[1].reshape(LEN, HEADS, HD), cosine, sine_table).astype(jnp.bfloat16)
        values_all = projected[2].reshape(LEN, HEADS, HD).astype(jnp.bfloat16)
        attn_probs = attention_probs(queries.astype(jnp.float32), keys_all.astype(jnp.float32), positions, seq_doc, seq_doc)
        probs_b = attn_probs.astype(jnp.bfloat16)
        attended = jnp.einsum('hqk,khd->qhd', probs_b.astype(jnp.float32), values_all.astype(jnp.float32)).reshape(LEN, D).astype(jnp.bfloat16)
        pre_act = jnp.dot(second_in, up_weight, preferred_element_type=jnp.float32) + up_bias.astype(jnp.float32)
        activated, gelu_slope = gelu_parts(pre_act)
        act_b = activated.astype(jnp.bfloat16)
        branches = jnp.dot(attended, out_weight, preferred_element_type=jnp.float32) + jnp.dot(act_b, down_weight, preferred_element_type=jnp.float32)
        out_rows = (seq_float + branches + out_bias.astype(jnp.float32) + down_bias.astype(jnp.float32)).astype(jnp.bfloat16)
        cot_float = seq_cot.astype(jnp.float32)
        bias_grad = lax.optimization_barrier(jnp.sum(cot_float, axis=0))
        grad_out_w = jnp.dot(attended.T, seq_cot, preferred_element_type=jnp.float32)
        grad_down_w = jnp.dot(act_b.T, seq_cot, preferred_element_type=jnp.float32)
        d_attended = jnp.dot(seq_cot, out_weight.T, preferred_element_type=jnp.float32).astype(jnp.bfloat16)
        d_pre = (jnp.dot(seq_cot, down_weight.T, preferred_element_type=jnp.float32) * gelu_slope).astype(jnp.bfloat16)
        grad_up_w = jnp.dot(second_in.T, d_pre, preferred_element_type=jnp.float32)
        grad_up_b = lax.optimization_barrier(jnp.sum(d_pre.astype(jnp.float32), axis=0))
        d_second = jnp.dot(d_pre, up_weight.T, preferred_element_type=jnp.float32)
        d_heads = d_attended.astype(jnp.float32).reshape(LEN, HEADS, HD)
        d_values = jnp.einsum('hqk,qhd->khd', probs_b.astype(jnp.float32), d_heads)
        d_probs = jnp.einsum('qhd,khd->hqk', d_heads, values_all.astype(jnp.float32))
        delta_sum = lax.optimization_barrier(jnp.sum(attn_probs * d_probs, axis=2, keepdims=True))
        d_scores = (attn_probs * (d_probs - delta_sum)).astype(jnp.bfloat16)
        d_query = jnp.einsum('hqk,khd->qhd', d_scores.astype(jnp.float32), keys_all.astype(jnp.float32)) * score_scale
        d_keys = jnp.einsum('hqk,qhd->khd', d_scores.astype(jnp.float32), queries.astype(jnp.float32)) * score_scale
        d_qkv = jnp.stack([rotate(d_query, cosine, -sine_table).reshape(LEN, D), rotate(d_keys, cosine, -sine_table).reshape(LEN, D), d_values.reshape(LEN, D)]).astype(jnp.bfloat16)
        grad_qkv_b = lax.optimization_barrier(jnp.sum(d_qkv.astype(jnp.float32), axis=1))
        grad_qkv_w = jnp.stack([jnp.dot(first_in.T, d_qkv[part_idx], preferred_element_type=jnp.float32) for part_idx in range(3)])
        d_first = jnp.dot(d_qkv[0], qkv_weight[0].T, preferred_element_type=jnp.float32)
        d_first = d_first + jnp.dot(d_qkv[1], qkv_weight[1].T, preferred_element_type=jnp.float32)
        d_first = d_first + jnp.dot(d_qkv[2], qkv_weight[2].T, preferred_element_type=jnp.float32)
        combined = d_first * gain_one + d_second * gain_two
        mean_one = lax.optimization_barrier(jnp.mean(combined, axis=1, keepdims=True))
        mean_two = lax.optimization_barrier(jnp.mean(combined * normed, axis=1, keepdims=True))
        grad_rows = (cot_float + inv_std * (combined - mean_one - normed * mean_two)).astype(jnp.bfloat16)
        terms = (grad_qkv_w, grad_qkv_b, grad_out_w, bias_grad, grad_up_w, grad_up_b, grad_down_w, lax.optimization_barrier(jnp.sum(d_first * normed, axis=0)), lax.optimization_barrier(jnp.sum(d_first, axis=0)), lax.optimization_barrier(jnp.sum(d_second * normed, axis=0)), lax.optimization_barrier(jnp.sum(d_second, axis=0)))
        new_totals = tuple((total + term for total, term in zip(totals, terms)))
        return (new_totals, (out_rows, grad_rows))
    start_totals = (jnp.zeros((3, D, D), jnp.float32), jnp.zeros((3, D), jnp.float32), jnp.zeros((D, D), jnp.float32), jnp.zeros((D,), jnp.float32), jnp.zeros((D, FF), jnp.float32), jnp.zeros((FF,), jnp.float32), jnp.zeros((FF, D), jnp.float32), jnp.zeros((D,), jnp.float32), jnp.zeros((D,), jnp.float32), jnp.zeros((D,), jnp.float32), jnp.zeros((D,), jnp.float32))
    sequences = (block_input.reshape(seq_count, LEN, D), cotangent.reshape(seq_count, LEN, D), doc_ids.reshape(seq_count, LEN), doc_start.reshape(seq_count, LEN))
    totals, stacked = lax.scan(one_sequence, start_totals, sequences)
    block_output = stacked[0].reshape(TOKENS, D)
    grad_input = stacked[1].reshape(TOKENS, D)
    return (block_output, grad_input, totals[0], totals[1], totals[2], totals[3], totals[4], totals[5], totals[6], totals[3], totals[7], totals[8], totals[9], totals[10])
```

```python
import jax
import jax.numpy as jnp
from jax import lax
from jax.experimental import pallas as pl
from jax.experimental.pallas import tpu as pltpu
import functools
import types
from jax.sharding import PartitionSpec as P

HD = 64
ROT = 16


EPS = 1e-05


def gelu_parts(pre_act):
    cumulative = 0.5 * (1.0 + jax.scipy.special.erf(pre_act * 0.7071067811865476))
    density = jnp.exp(-0.5 * pre_act * pre_act) * 0.3989422804014327
    return (pre_act * cumulative, cumulative + pre_act * density)


def angle_tables(offsets):
    half_rot = ROT // 2
    frequency = 10000.0 ** (-(2.0 * jnp.arange(half_rot, dtype=jnp.float32)) / ROT)
    angles = offsets.astype(jnp.float32)[:, None] * frequency[None, :]
    angles = jnp.concatenate([angles, angles], axis=1)
    return (jnp.cos(angles), jnp.sin(angles))


def rotate(tensor, cosine, sine_table):
    half_rot = ROT // 2
    turned = jnp.concatenate([-tensor[..., half_rot:ROT], tensor[..., :half_rot]], axis=-1)
    leading = tensor[..., :ROT] * cosine[:, None, :] + turned * sine_table[:, None, :]
    return jnp.concatenate([leading, tensor[..., ROT:]], axis=-1)


def normalize(rows_in):
    centered = rows_in - jnp.mean(rows_in, axis=1, keepdims=True)
    inv_std = lax.rsqrt(jnp.mean(centered * centered, axis=1, keepdims=True) + EPS)
    return (centered * inv_std, inv_std)


MESH = pl.DeviceIdType.MESH
VMEM = pl.BlockSpec(memory_space=pltpu.VMEM)
ANY = pl.BlockSpec(memory_space=pl.ANY)
PLANE = ("fsdp", "ctx")


def position():
    f = lax.axis_index("fsdp")
    return lax.rem(f, 2), f // 2, lax.axis_index("ctx"), lax.axis_index("tp")


def partner():
    core, y, _, _ = position()
    return {"fsdp": y * 2 + 1 - core}


def x_peer():
    return {"ctx": 1 - lax.axis_index("ctx")}


def y_peer():
    core, y, _, _ = position()
    return {"fsdp": (1 - y) * 2 + core}


def plane_peer(step):
    rank = lax.rem(lax.axis_index("fsdp") * 2 + lax.axis_index("ctx") + step, 8)
    return {"fsdp": rank // 2, "ctx": lax.rem(rank, 2)}


def z_peer(step, count):
    return {"tp": lax.rem(lax.axis_index("tp") + step, count)}


def greet(peers):
    barrier = pltpu.get_barrier_semaphore()
    for peer in peers:
        pl.semaphore_signal(barrier, inc=1, device_id=peer, device_id_type=MESH)
    pl.semaphore_wait(barrier, len(peers))


def remote(src, dst, sems, k, peer):
    return pltpu.make_async_remote_copy(
        src_ref=src,
        dst_ref=dst,
        send_sem=sems[0].at[k],
        recv_sem=sems[1].at[k],
        device_id=peer,
        device_id_type=MESH,
    )


def run_all(*parts):
    parts = list(parts)
    while parts:
        parts = [part for part in parts if next(part, "end") != "end"]


def plane_gather(src, out, sems, own_sem):
    core, y, x, _ = position()
    half = src.shape[0] // 2
    first, second = pl.ds(0, half), pl.ds(half, half)

    def slot(yy, xx):
        return (yy * 2 + core) * 2 + xx

    own, from_x, from_y, diag = slot(y, x), slot(y, 1 - x), slot(1 - y, x), slot(1 - y, 1 - x)
    to_p, to_x, to_y = partner(), x_peer(), y_peer()

    def piece(k, where, rows, peer):
        place = out.at[where, rows]
        return remote(src.at[rows] if k < 4 else place, place, sems, k, peer)

    sends = [
        piece(0, own, first, to_x),
        piece(1, own, second, to_y),
        piece(2, own, second, to_x),
        piece(3, own, first, to_y),
    ]
    whole = remote(src, out.at[own], sems, 4, to_p)
    keep = pltpu.make_async_copy(src, out.at[own], own_sem)
    for copy in sends:
        copy.start()
    whole.start()
    keep.start()
    yield
    relays = [
        (0, [(5, from_x, first, to_y), (7, from_x, first, to_p)]),
        (1, [(6, from_y, second, to_x), (8, from_y, second, to_p)]),
        (2, [(9, from_x, second, to_p)]),
        (3, [(10, from_y, first, to_p)]),
    ]
    later = []
    for k, nexts in relays:
        sends[k].wait_recv()
        for args in nexts:
            copy = piece(*args)
            copy.start()
            later.append(copy)
        if k == 1:
            yield
    by_key = {5: later[0], 6: later[2]}
    yield
    for k, args in ((5, (11, diag, first, to_p)), (6, (12, diag, second, to_p))):
        by_key[k].wait_recv()
        copy = piece(*args)
        copy.start()
        later.append(copy)
    yield
    for copy in later:
        if copy is not by_key[5] and copy is not by_key[6]:
            copy.wait_recv()
    whole.wait_recv()
    for copy in sends + later + [whole]:
        copy.wait_send()
    keep.wait()


def z_gather(src, out, ups, downs, own_sem, count):
    t = lax.axis_index("tp")
    keep = pltpu.make_async_copy(src, out.at[t], own_sem)

    def up(s):
        where = out.at[jnp.maximum(t - s, 0)]
        peer = {"tp": jnp.minimum(t + 1, count - 1)}
        return remote(src if s == 0 else where, where, ups, s, peer)

    def down(s):
        where = out.at[jnp.minimum(t + s, count - 1)]
        peer = {"tp": jnp.maximum(t - 1, 0)}
        return remote(src if s == 0 else where, where, downs, s, peer)

    for s in range(count):
        if s > 0:

            @pl.when(t - s >= 0)
            def _():
                up(s - 1).wait_recv()

            @pl.when(t + s <= count - 1)
            def _():
                down(s - 1).wait_recv()

        if s < count - 1:

            @pl.when((t - s >= 0) & (t < count - 1))
            def _():
                up(s).start()

            @pl.when((t + s <= count - 1) & (t > 0))
            def _():
                down(s).start()

            if s == 0:
                keep.start()
            yield
    for s in range(count - 1):

        @pl.when((t - s >= 0) & (t < count - 1))
        def _():
            up(s).wait_send()

        @pl.when((t + s <= count - 1) & (t > 0))
        def _():
            down(s).wait_send()

    keep.wait()


def x_gather(src, out, sems, own_sem):
    x = lax.axis_index("ctx")
    copy = remote(src, out.at[x], sems, 0, x_peer())
    keep = pltpu.make_async_copy(src, out.at[x], own_sem)
    copy.start()
    keep.start()
    yield
    yield
    yield
    copy.wait()
    keep.wait()


def x_swap(src, out, sems):
    copy = remote(src.at[1 - lax.axis_index("ctx")], out, sems, 0, x_peer())
    copy.start()
    yield
    yield
    copy.wait()


def plane_scatter(src, out, core_in, summed, side_in, mixed, last_in, sems):
    core, y, x, _ = position()
    half = out.shape[0] // 2
    rows = (pl.ds(0, half), pl.ds(half, half))
    to_p, to_x, to_y = partner(), x_peer(), y_peer()
    wide = jnp.float32
    first = []
    for q in range(4):
        there = ((q // 2) * 2 + 1 - core) * 2 + q % 2
        first.append(remote(src.at[there], core_in.at[q], sems, q, to_p))
    for copy in first:
        copy.start()
    yield
    for q in range(4):
        first[q].wait_recv()
        here = ((q // 2) * 2 + core) * 2 + q % 2
        summed[q] = (src[here].astype(wide) + core_in[q].astype(wide)).astype(summed.dtype)
    second = [
        remote(summed.at[(1 - y) * 2 + 1 - x, rows[0]], side_in.at[0], sems, 4, to_x),
        remote(summed.at[(1 - y) * 2 + 1 - x, rows[1]], side_in.at[1], sems, 5, to_y),
        remote(summed.at[y * 2 + 1 - x, rows[0]], side_in.at[2], sems, 6, to_x),
        remote(summed.at[(1 - y) * 2 + x, rows[1]], side_in.at[3], sems, 7, to_y),
    ]
    for copy in second:
        copy.start()
    yield
    third = []
    for k, (where, peer) in enumerate((((1 - y) * 2 + x, to_y), (y * 2 + 1 - x, to_x))):
        second[k].wait_recv()
        total = summed[where, rows[k]].astype(wide) + side_in[k].astype(wide)
        mixed[k] = total.astype(mixed.dtype)
        copy = remote(mixed.at[k], last_in.at[k], sems, 8 + k, peer)
        copy.start()
        third.append(copy)
    yield
    for k in range(2):
        second[2 + k].wait_recv()
        third[k].wait_recv()
        out[rows[k]] = (
            summed[y * 2 + x, rows[k]].astype(wide)
            + side_in[2 + k].astype(wide)
            + last_in[k].astype(wide)
        )
    for copy in first + second + third:
        copy.wait_send()


def z_scatter(src, out, landed, sems, count):
    t = lax.axis_index("tp")
    copies = []
    for d in range(1, count):
        peer = z_peer(d, count)
        copies.append(remote(src.at[peer["tp"]], landed.at[d - 1], sems, d - 1, peer))
    for copy in copies:
        copy.start()
    yield
    yield
    yield
    total = src[t].astype(jnp.float32)
    for d in range(1, count):
        copies[d - 1].wait()
        total = total + landed[d - 1].astype(jnp.float32)
    out[...] = total


def small_sum(src, out, z_in, middle, plane_in, z_sems, plane_sems, count, shared):
    t = lax.axis_index("tp")
    rank = lax.axis_index("fsdp") * 2 + lax.axis_index("ctx")
    ones = [remote(src, z_in.at[t], z_sems, d - 1, z_peer(d, count)) for d in range(1, count)]
    for copy in ones:
        copy.start()
    z_in[t] = src[...]
    yield
    for copy in ones:
        copy.wait()
    total = z_in[0]
    for i in range(1, count):
        total = total + z_in[i]
    row = lax.broadcasted_iota(jnp.int32, total.shape, 0)
    middle[...] = jnp.where(row < shared, total, src[...])
    twos = [remote(middle, plane_in.at[rank], plane_sems, d - 1, plane_peer(d)) for d in range(1, 8)]
    for copy in twos:
        copy.start()
    plane_in[rank] = middle[...]
    yield
    yield
    for copy in twos:
        copy.wait()
    total = plane_in[0]
    for i in range(1, 8):
        total = total + plane_in[i]
    out[...] = total


def near_peers(count):
    return [partner(), x_peer(), y_peer()] + [z_peer(d, count) for d in range(1, count)]


def sem_pair(count):
    return [pltpu.SemaphoreType.DMA((count,)), pltpu.SemaphoreType.DMA((count,))]


def call(body, outs, out_specs, inputs, scratch, collective):
    return pl.pallas_call(
        body,
        out_shape=outs,
        in_specs=[VMEM] * len(inputs),
        out_specs=out_specs,
        scratch_shapes=scratch,
        compiler_params=pltpu.CompilerParams(
            collective_id=collective, has_side_effects=True, vmem_limit_bytes=48 * 1024 * 1024
        ),
    )(*inputs)


def shape(dims, dtype=jnp.bfloat16):
    return jax.ShapeDtypeStruct(dims, dtype)


def ready(generator):
    return next(generator, "end")


def lanes(dims):
    return lax.broadcasted_iota(jnp.int32, dims, len(dims) - 1)


def rotate_tile(tile, tables, sign):
    turned = pltpu.roll(tile, 128 - ROT // 2, 1) * tables[1] + pltpu.roll(tile, ROT // 2, 1) * tables[2]
    return tile * tables[0] + sign * turned


def fused_kernel(names, count, *refs):
    r = types.SimpleNamespace(**dict(zip(names, refs)))
    wide, narrow = jnp.float32, jnp.bfloat16
    _, _, x, t = position()
    row_count, width = r.normed.shape
    heads_here = r.qs.shape[0]
    own_count = row_count // count
    piece = r.pack_a.shape[0]
    lw = heads_here * HD
    block = min(256, row_count)
    blocks = row_count // block
    last, rows = ((1,), (1,)), ((0,), (0,))
    half_rot = ROT // 2
    params = r.params
    hidden = r.wu.shape[2]
    kv_sem = (r.kv_send, r.kv_recv)
    far_sem = (r.far_send, r.far_recv)

    def span(b):
        return pl.ds(pl.multiple_of(b * block, block), block)

    def each_block(step):
        lax.fori_loop(0, blocks, lambda b, _: (step(b), 0)[1], 0)

    def pair(name):
        return (getattr(r, name + "_s"), getattr(r, name + "_r"))

    def square(ref):
        return ref[...].reshape(ref.shape[0] * ref.shape[1], ref.shape[2])

    loads = [
        pltpu.make_async_copy(a, b, r.load.at[k])
        for k, (a, b) in enumerate(
            (
                (r.qkv, r.raw_qkv),
                (r.outw, r.raw_out),
                (r.qkv_bias, r.raw_bias),
                (r.doc_start, r.raw_start),
                (r.gain_one, r.v_gain_one),
                (r.bias_one, r.v_bias_one),
                (r.gain_two, r.v_gain_two),
                (r.bias_two, r.v_bias_two),
                (r.up_bias, r.v_up_bias),
                (r.out_bias, r.v_out_bias),
                (r.down_bias, r.v_down_bias),
            )
        )
    ]
    for copy in loads:
        copy.start()
    greet([plane_peer(i) for i in range(1, 8)] + [z_peer(i, count) for i in range(1, count)])
    zr = z_gather(r.rows, r.full_in, pair("zru"), pair("zrd"), r.own.at[0], count)
    zc = z_gather(r.cot, r.full_cot, pair("zcu"), pair("zcd"), r.own.at[1], count)
    ga = plane_gather(r.pack_a, r.wa, pair("ga"), r.own.at[2])
    gu = plane_gather(r.up, r.wu, pair("gu"), r.own.at[3])
    gd = plane_gather(r.down, r.wd, pair("gd"), r.own.at[4])
    ready(zr)

    def turn_over(value):
        n = value.shape[1]
        one = (lax.broadcasted_iota(jnp.int32, (n, n), 0) == lanes((n, n))).astype(narrow)
        return dot(one, value, last).astype(narrow)

    loads[0].wait()
    loads[1].wait()
    out_t = turn_over(r.raw_out[...])
    tiles = []
    for h in range(heads_here):
        cut = slice(h * HD, (h + 1) * HD)
        tiles += [r.raw_qkv[1][:, cut], r.raw_qkv[2][:, cut]]
    for h in range(heads_here):
        cut = slice(h * HD, (h + 1) * HD)
        tiles += [r.raw_qkv[0][:, cut], out_t[:, cut]]
    r.pack_a[...] = jnp.concatenate(tiles, axis=1)
    ready(ga)
    ready(gu)
    for copy in loads[2:]:
        copy.wait()

    def row_of(ref):
        return ref[...].astype(wide).reshape(1, ref.shape[0])

    params[...] = jnp.zeros_like(params)
    params[0:1, :width] = row_of(r.v_gain_one)
    params[1:2, :width] = row_of(r.v_bias_one)
    params[2:3, :width] = row_of(r.v_gain_two)
    params[3:4, :width] = row_of(r.v_bias_two)
    bias = r.raw_bias[...].astype(wide)
    tiles = []
    for h in range(heads_here):
        cut = slice(h * HD, (h + 1) * HD)
        tiles += [bias[1:2, cut], bias[2:3, cut]]
    for h in range(heads_here):
        tiles += [bias[0:1, h * HD : (h + 1) * HD], jnp.zeros((1, HD), wide)]
    params[4:5, : 4 * lw] = jnp.concatenate(tiles, axis=1)
    params[5:6, :hidden] = row_of(r.v_up_bias)
    params[6:7, :width] = row_of(r.v_out_bias) + row_of(r.v_down_bias)

    lane = lanes((8, 128))
    sub = lax.broadcasted_iota(jnp.int32, (8, 128), 0)
    is_key = lane < HD
    low = ((lane == sub) & is_key).astype(wide)
    high = ((lane == sub + half_rot) & is_key).astype(wide)

    def expand(value, table):
        return lax.dot_general(
            value, table, (rows, ((), ())), precision=lax.Precision.HIGHEST, preferred_element_type=wide
        )

    start = jnp.broadcast_to(r.raw_start[...].reshape(1, row_count), (half_rot, row_count))
    dims = (half_rot, row_count)
    which = lax.broadcasted_iota(jnp.int32, dims, 0)
    frequency = jnp.zeros(dims, wide)
    for i in range(half_rot):
        frequency = jnp.where(which == i, 10000.0 ** (-2.0 * i / ROT), frequency)
    angles = (x * row_count + lanes(dims) - start).astype(wide) * frequency
    rest = (lanes((1, 128)) >= ROT).astype(wide)
    r.tables[0] = expand(jnp.cos(angles), low + high) + rest
    r.tables[1] = expand(jnp.sin(angles), -low)
    r.tables[2] = expand(jnp.sin(angles), high)
    r.start[...] = expand(start.astype(wide), (sub == 0).astype(wide))
    key_scale = (lanes((1, 128)) < HD).astype(wide) * HD ** (-0.5)
    value_mask = (lanes((1, 128)) >= HD).astype(wide)

    ready(ga)
    ready(zr)
    ready(ga)
    ready(gu)
    ready(gd)
    ready(zr)
    ready(zc)
    ready(ga)
    ready(gu)
    ready(zr)
    ready(ga)

    def norm_chunk(c, _):
        values = r.full_in[c].astype(wide)
        normed, inv_std = normalize(values)
        where = pl.ds(pl.multiple_of(c * own_count, own_count), own_count)
        r.normed[where] = normed
        r.inv[where] = jnp.broadcast_to(inv_std, (own_count, 128))
        r.first[where] = (normed * params[0:1, :width] + params[1:2, :width]).astype(narrow)
        r.second[where] = (normed * params[2:3, :width] + params[3:4, :width]).astype(narrow)
        return 0

    lax.fori_loop(0, count, norm_chunk, 0)

    def tables_at(b):
        return [r.tables[k, span(b)] for k in range(3)]

    def project(b):
        tabs = tables_at(b)
        out = dot(r.first[span(b)], square(r.wa)) + params[4:5, : 4 * lw]
        where = pl.ds(pl.multiple_of(x * row_count + b * block, block), block)
        for h in range(heads_here):
            tile = out[:, h * 128 : (h + 1) * 128]
            r.kv[h, where] = rotate_tile(tile, tabs, 1.0).astype(narrow)
            tile = out[:, (heads_here + h) * 128 : (heads_here + h + 1) * 128]
            r.qs[h, span(b)] = (rotate_tile(tile, tabs, 1.0) * key_scale).astype(narrow)

    each_block(project)
    early = r.kv.at[:, pl.ds(0, row_count)]
    kv_copy = remote(early, early, kv_sem, 0, x_peer())

    @pl.when(x == 0)
    def _():
        kv_copy.start()

    ready(gu)
    ready(gd)
    ready(zc)

    def up(b):
        pre = dot(r.second[span(b)], square(r.wu)) + params[5:6, :hidden]
        activated, slope = gelu_parts(pre)
        r.act[span(b)] = activated.astype(narrow)
        r.slope[span(b)] = slope

    ready(gu)
    each_block(up)
    ready(gd)
    ready(zc)
    ready(gd)
    ready(gd)

    def down(b):
        r.forward[span(b)] = dot(r.act[span(b)], square(r.wd), last)

    each_block(down)

    @pl.when(x == 1)
    def _():
        kv_copy.wait_recv()

    def attend(side):
        def head(h, _):
            for b in range(blocks):
                keys = side * row_count + (b + 1) * block
                cut = pl.ds(b * block, block)
                kv = r.kv[h, pl.ds(0, keys)]
                scores = dot(r.qs[h, cut], kv, last)
                key_pos = lanes((block, keys))
                query_pos = side * row_count + b * block + lax.broadcasted_iota(jnp.int32, (block, keys), 0)
                start = r.start[cut, 0:1].astype(jnp.int32)
                allowed = (key_pos >= start) & (key_pos <= query_pos)
                scores = jnp.where(allowed, scores, -1e30)
                exponent = jnp.exp(scores - jnp.max(scores, axis=1, keepdims=True))
                probs = exponent * (1.0 / jnp.sum(exponent, axis=1, keepdims=True))
                r.probs[h, cut, pl.ds(0, keys)] = probs
                r.attz[h, cut] = (dot(probs.astype(narrow), kv) * value_mask).astype(narrow)
            return 0

        lax.fori_loop(0, heads_here, head, 0)

    for side in range(2):
        pl.when(x == side)(functools.partial(attend, side))

    @pl.when(x == 0)
    def _():
        kv_copy.wait_send()

    ready(zc)

    def heads_of(ref, where):
        return jnp.concatenate([ref[h, where] for h in range(heads_here)], axis=1)

    def chunks(b):
        per = block // own_count
        return pl.ds(b * per, per)

    query_cut = slice(2 * lw, 4 * lw)

    def finish_forward(b):
        weight = square(r.wa)[:, query_cut]
        total = r.forward[span(b)] + dot(heads_of(r.attz, span(b)), weight, last)
        r.fs_src[chunks(b)] = total.astype(narrow).reshape(block // own_count, own_count, width)

    each_block(finish_forward)
    fs = z_scatter(r.fs_src, r.fs_sum, r.fs_land, pair("fs"), count)
    ready(fs)

    def cot_rows(b):
        return r.full_cot[chunks(b)].reshape(block, width)

    r.small_src[...] = jnp.zeros_like(r.small_src)

    def before(b):
        cot = cot_rows(b)
        d_pre = (dot(cot, square(r.wd)) * r.slope[span(b)]).astype(narrow)
        r.d_pre[span(b)] = d_pre
        r.small_src[5:6, : d_pre.shape[1]] += jnp.sum(d_pre.astype(wide), axis=0, keepdims=True)
        d_att = dot(cot, square(r.wa)[:, query_cut])
        for h in range(heads_here):
            r.az[h, span(b)] = (d_att[:, h * 128 : (h + 1) * 128] * value_mask).astype(narrow)

    each_block(before)
    cot_all = square(r.full_cot)
    group = r.gu_src.shape[0]

    def to_pieces(value):
        return value.astype(narrow).reshape(group, piece, value.shape[1])

    r.gu_src[...] = to_pieces(dot(r.second[...], r.d_pre[...], rows))

    def scatter(name, out):
        parts = [getattr(r, name + k) for k in "abcde"]
        return plane_scatter(getattr(r, name + "_src"), out, *parts, pair(name + "s"))

    su, sd, sa = scatter("gu", r.sum_u), scatter("gd", r.sum_d), scatter("ga", r.sum_a)
    ready(su)
    r.gd_src[...] = to_pieces(dot(cot_all, r.act[...], rows))
    ready(sd)

    def second_back(b):
        d_second = dot(r.d_pre[span(b)], square(r.wu), last)
        r.small_src[3:4, :width] += jnp.sum(d_second * r.normed[span(b)], axis=0, keepdims=True)
        r.small_src[4:5, :width] += jnp.sum(d_second, axis=0, keepdims=True)
        r.d_second[span(b)] = d_second * params[2:3, :width]

    each_block(second_back)
    ready(su)
    ready(sd)

    def far(h):
        return remote(r.far_src.at[h], r.far_in.at[h], far_sem, h, x_peer())

    def attend_back(side):
        def head(h, _):
            for b in reversed(range(blocks)):
                keys = side * row_count + (b + 1) * block
                cut, used = pl.ds(b * block, block), pl.ds(0, keys)
                probs, kv = r.probs[h, cut, used], r.kv[h, used]
                d_att, query = r.az[h, cut], r.qs[h, cut]
                d_probs = dot(d_att, kv, last)
                delta = jnp.sum(probs * d_probs, axis=1, keepdims=True)
                d_scores = (probs * (d_probs - delta)).astype(narrow)
                d_query = rotate_tile(dot(d_scores, kv), [r.tables[k, cut] for k in range(3)], -1.0)
                r.d_query[h, cut] = (d_query * key_scale).astype(narrow)
                grads = dot(d_scores, query, rows) + dot(probs.astype(narrow), d_att, rows)
                if b == blocks - 1:
                    r.d_kv[h, used] = grads
                else:
                    r.d_kv[h, used] += grads
            if side == 1:
                r.far_src[h] = r.d_kv[h, pl.ds(0, row_count)].astype(narrow)
                far(h).start()
            return 0

        lax.fori_loop(0, heads_here, head, 0)

    for side in range(2):
        pl.when(x == side)(functools.partial(attend_back, side))
    ready(su)
    ready(sd)
    for h in range(heads_here):

        @pl.when(x == 0)
        def _():
            far(h).wait_recv()
            r.d_kv[h, pl.ds(0, row_count)] += r.far_in[h].astype(wide)

    def gather_grads(b):
        tabs = tables_at(b)
        where = pl.ds(pl.multiple_of(x * row_count + b * block, block), block)
        for h in range(heads_here):
            value = rotate_tile(r.d_kv[h, where], tabs, -1.0).astype(narrow)
            r.d_pack[span(b), h * 128 : (h + 1) * 128] = value
            cut = slice((heads_here + h) * 128, (heads_here + h + 1) * 128)
            r.d_pack[span(b), cut] = r.d_query[h, span(b)]
        d_pack = r.d_pack[span(b)]
        r.small_src[6:7, : 4 * lw] += jnp.sum(d_pack.astype(wide), axis=0, keepdims=True)
        d_first = dot(d_pack, square(r.wa), last)
        r.small_src[1:2, :width] += jnp.sum(d_first * r.normed[span(b)], axis=0, keepdims=True)
        r.small_src[2:3, :width] += jnp.sum(d_first, axis=0, keepdims=True)
        total = d_first * params[0:1, :width] + r.d_second[span(b)]
        r.gs_src[chunks(b)] = total.astype(narrow).reshape(block // own_count, own_count, width)

    each_block(gather_grads)
    gs = z_scatter(r.gs_src, r.gs_sum, r.gs_land, pair("gs"), count)
    ready(gs)
    cot_own = r.full_cot[t].astype(wide)
    r.small_src[0:1, :width] = jnp.sum(cot_own, axis=0, keepdims=True)
    sm = small_sum(
        r.small_src, r.small_sum, r.small_z, r.small_mid, r.small_p,
        pair("smz"), pair("smp"), count, 5,
    )
    ready(sm)
    first_all = r.first[...]
    r.ga_src[:, :, : 2 * lw] = to_pieces(dot(first_all, r.d_pack[:, : 2 * lw], rows))
    mixed = dot(first_all, r.d_pack[:, query_cut], rows)
    mixed += dot(cot_all, heads_of(r.attz, slice(None)), rows)
    r.ga_src[:, :, query_cut] = to_pieces(mixed)
    ready(sa)
    ready(su)
    ready(sd)
    for _ in range(3):
        ready(fs)
    base = r.full_in[t].astype(wide) + r.fs_sum[...]
    r.v_rows[...] = (base + params[6:7, :width]).astype(narrow)
    results = [
        pltpu.make_async_copy(a, b, r.store.at[k])
        for k, (a, b) in enumerate(
            (
                (r.v_rows, r.out_rows),
                (r.sum_u, r.out_u),
                (r.sum_d, r.out_d),
                (r.v_qkv, r.out_qkv),
                (r.v_out, r.out_out),
                (r.v_grad, r.out_grad),
                (r.small_sum, r.out_small),
                (r.v_bias, r.out_bias_qkv),
            )
        )
    ]
    for copy in results[:3]:
        copy.start()
    ready(sa)
    ready(sm)
    ready(sa)
    ready(sm)
    ready(sa)

    def split_tiles(value):
        halves = [value[:, k * HD : (k + 1) * HD] for k in range(4 * heads_here)]
        keys, values = halves[0 : 2 * heads_here : 2], halves[1 : 2 * heads_here : 2]
        return [jnp.concatenate(v, axis=1) for v in (halves[2 * heads_here :: 2], keys, values)]

    total = r.sum_a[...]
    for k, value in enumerate(split_tiles(total)):
        r.v_qkv[k] = value
    one = lax.broadcasted_iota(jnp.int32, (piece, piece), 0) == lanes((piece, piece))
    for h in range(heads_here):
        cut = slice((heads_here + h) * 128, (heads_here + h + 1) * 128)
        r.v_out[h * HD : (h + 1) * HD] = expand(total[:, cut], one.astype(wide))[HD:]
    results[3].start()
    results[4].start()
    ready(sm)
    for k, value in enumerate(split_tiles(r.small_sum[6:7, : 4 * lw])):
        r.v_bias[k : k + 1] = value
    results[6].start()
    results[7].start()
    for _ in range(3):
        ready(gs)
    mine = pl.ds(pl.multiple_of(t * own_count, own_count), own_count)
    combined, normed = r.gs_sum[...], r.normed[mine]
    mean_one = jnp.mean(combined, axis=1, keepdims=True)
    mean_two = jnp.mean(combined * normed, axis=1, keepdims=True)
    grad = cot_own + r.inv[mine, 0:1] * (combined - mean_one - normed * mean_two)
    r.v_grad[...] = grad.astype(narrow)
    results[5].start()

    @pl.when(x == 1)
    def _():
        for h in range(heads_here):
            far(h).wait_send()

    for copy in results:
        copy.wait()
    run_all(zr, zc, ga, gu, gd, su, sd, sa, fs, gs, sm)


def fused_call(arrays, count):
    own, width = arrays["rows"].shape
    piece, hidden = arrays["up"].shape
    lw = arrays["qkv"].shape[2]
    heads = lw // HD
    row_count = own * count
    group = 8
    wide, narrow = jnp.float32, jnp.bfloat16
    pack = 4 * lw
    small = (8, max(width, hidden, pack))
    outs = dict(
        out_rows=((own, width), narrow),
        out_grad=((own, width), narrow),
        out_qkv=((3, piece, lw), wide),
        out_out=((lw, piece), wide),
        out_u=((piece, hidden), wide),
        out_d=((piece, hidden), wide),
        out_small=(small, wide),
        out_bias_qkv=((3, lw), wide),
    )
    scratch = dict(
        raw_qkv=(arrays["qkv"].shape, narrow),
        raw_out=(arrays["outw"].shape, narrow),
        raw_bias=((3, lw), narrow),
        raw_start=((row_count,), jnp.int32),
        v_gain_one=((width,), narrow),
        v_bias_one=((width,), narrow),
        v_gain_two=((width,), narrow),
        v_bias_two=((width,), narrow),
        v_up_bias=((hidden,), narrow),
        v_out_bias=((width,), narrow),
        v_down_bias=((width,), narrow),
        params=(small, wide),
        sum_a=((piece, pack), wide),
        sum_u=((piece, hidden), wide),
        sum_d=((piece, hidden), wide),
        small_sum=(small, wide),
        v_rows=((own, width), narrow),
        v_grad=((own, width), narrow),
        v_qkv=((3, piece, lw), wide),
        v_out=((lw, piece), wide),
        v_bias=((3, lw), wide),
        pack_a=((piece, pack), narrow),
        wa=((group, piece, pack), narrow),
        wu=((group, piece, hidden), narrow),
        wd=((group, piece, hidden), narrow),
        full_in=((count, own, width), narrow),
        full_cot=((count, own, width), narrow),
        tables=((3, row_count, 128), wide),
        start=((row_count, 128), wide),
        normed=((row_count, width), wide),
        inv=((row_count, 128), wide),
        first=((row_count, width), narrow),
        second=((row_count, width), narrow),
        kv=((heads, 2 * row_count, 128), narrow),
        qs=((heads, row_count, 128), narrow),
        az=((heads, row_count, 128), narrow),
        attz=((heads, row_count, 128), narrow),
        act=((row_count, hidden), narrow),
        slope=((row_count, hidden), wide),
        forward=((row_count, width), wide),
        probs=((heads, row_count, 2 * row_count), wide),
        d_pre=((row_count, hidden), narrow),
        d_second=((row_count, width), wide),
        d_query=((heads, row_count, 128), narrow),
        d_kv=((heads, 2 * row_count, 128), wide),
        far_src=((heads, row_count, 128), narrow),
        far_in=((heads, row_count, 128), narrow),
        d_pack=((row_count, pack), narrow),
        fs_src=((count, own, width), narrow),
        fs_land=((count - 1, own, width), narrow),
        fs_sum=((own, width), wide),
        gs_src=((count, own, width), narrow),
        gs_land=((count - 1, own, width), narrow),
        gs_sum=((own, width), wide),
        small_src=(small, wide),
        small_z=((count,) + small, wide),
        small_mid=(small, wide),
        small_p=((group,) + small, wide),
    )
    half = piece // 2
    for name, span in dict(ga=pack, gu=hidden, gd=hidden).items():
        scratch[name + "_src"] = ((group, piece, span), narrow)
        for k, dims in zip("abcde", ((4, piece), (4, piece), (4, half), (2, half), (2, half))):
            scratch[name + k] = (dims + (span,), narrow)
    sems = dict(load=11, store=8, own=5, kv_send=1, kv_recv=1, far_send=heads, far_recv=heads)
    z = count - 1
    pairs = dict(zru=z, zrd=z, zcu=z, zcd=z, fs=z, gs=z, smz=z, smp=7)
    pairs.update(ga=13, gu=13, gd=13, gas=10, gus=10, gds=10)
    for name, number in pairs.items():
        sems[name + "_s"] = sems[name + "_r"] = number
    names = list(arrays) + list(outs) + list(scratch) + list(sems)
    buffers = [pltpu.VMEM(dims, kind) for dims, kind in scratch.values()]
    buffers += [pltpu.SemaphoreType.DMA((number,)) for number in sems.values()]
    return pl.pallas_call(
        functools.partial(fused_kernel, names, count),
        out_shape=[shape(dims, kind) for dims, kind in outs.values()],
        in_specs=[ANY] * len(arrays),
        out_specs=[ANY] * len(outs),
        scratch_shapes=buffers,
        compiler_params=pltpu.CompilerParams(
            collective_id=0, has_side_effects=True, vmem_limit_bytes=60 * 1024 * 1024
        ),
    )(*arrays.values())


def last_call(given, width, hidden):
    def body(*refs):
        small, bias = refs[6], refs[7]
        given, outs, sem = refs[:6], refs[8:22], refs[22]
        places = (0, 1, 2, 4, 6, 8)
        copies = [
            pltpu.make_async_copy(src, outs[k], sem.at[i])
            for i, (src, k) in enumerate(zip(given, places))
        ]
        for copy in copies:
            copy.start()
        outs[3][...] = bias[...]
        for k, row in ((5, 0), (9, 0), (10, 1), (11, 2), (12, 3), (13, 4)):
            outs[k][...] = small[row, :width]
        outs[7][...] = small[5, :hidden]
        for copy in copies:
            copy.wait()

    wide = jnp.float32
    vector = shape((width,), wide)
    shapes = [shape(v.shape, v.dtype) for v in given]
    outs = shapes[:3] + [shapes[7], shapes[3], vector, shapes[4], shape((hidden,), wide), shapes[5]]
    outs += [vector] * 5
    specs = [ANY] * 3 + [VMEM, ANY, VMEM, ANY, VMEM, ANY] + [VMEM] * 5
    return pl.pallas_call(
        body,
        out_shape=outs,
        in_specs=[VMEM] * 8,
        out_specs=specs,
        scratch_shapes=[pltpu.SemaphoreType.DMA((6,))],
        compiler_params=pltpu.CompilerParams(vmem_limit_bytes=60 * 1024 * 1024),
    )(*given)


def fused_local(
    sizes,
    block_input,
    cotangent,
    norm1_gain,
    norm1_bias,
    norm2_gain,
    norm2_bias,
    qkv_weight,
    qkv_bias,
    out_weight,
    out_bias,
    up_weight,
    up_bias,
    down_weight,
    down_bias,
    doc_ids,
    doc_start,
):
    count = sizes[2]
    arrays = dict(rows=block_input, cot=cotangent, up=up_weight, qkv=qkv_weight, outw=out_weight)
    arrays.update(down=down_weight.T, gain_one=norm1_gain, bias_one=norm1_bias)
    arrays.update(gain_two=norm2_gain, bias_two=norm2_bias, up_bias=up_bias, out_bias=out_bias)
    arrays.update(down_bias=down_bias, qkv_bias=qkv_bias, doc_start=doc_start)
    out = list(last_call(fused_call(arrays, count), block_input.shape[1], up_bias.shape[0]))
    out[8] = out[8].T
    return tuple(out)


def plain_gather_first(weights, rows, count):
    return lax.all_gather(weights, PLANE), lax.all_gather(rows, "tp")


def plain_gather_second(rows, keys, count):
    return lax.all_gather(rows, "tp"), lax.all_gather(keys, "ctx")


def plain_scatter(grads, partial):
    grads = lax.psum_scatter(grads.astype(jnp.float32), PLANE, scatter_dimension=0)
    return grads, lax.psum_scatter(partial.astype(jnp.float32), "tp", scatter_dimension=0)


def plain_scatter_first(grads, partial, key_grads, count):
    x = lax.axis_index("ctx")
    total = lax.psum_scatter(key_grads.astype(jnp.float32), "ctx", scatter_dimension=0)
    own = lax.dynamic_index_in_dim(key_grads, x, 0, keepdims=False)
    return plain_scatter(grads, partial) + (total - own.astype(jnp.float32),)


def plain_scatter_second(grads, partial, small, count, shared):
    total = lax.psum(small, PLANE)
    return plain_scatter(grads, partial) + (
        jnp.concatenate([lax.psum(total[:shared], "tp"), total[shared:]]),
    )


def attention_probs(queries, keys_all, query_pos, query_start):
    score_scale = HD ** (-0.5)
    scores = (
        jnp.einsum("qhd,khd->hqk", queries, keys_all, preferred_element_type=jnp.float32)
        * score_scale
    )
    key_pos = jnp.arange(keys_all.shape[0], dtype=jnp.int32)
    allowed = (key_pos[None, :] >= query_start[:, None]) & (key_pos[None, :] <= query_pos[:, None])
    masked = jnp.where(allowed[None], scores, -1e30)
    row_peak = jnp.max(masked, axis=2, keepdims=True)
    exponent = jnp.where(allowed[None], jnp.exp(masked - row_peak), 0.0)
    return exponent / jnp.sum(exponent, axis=2, keepdims=True)


def dot(a, b, dims=((1,), (0,))):
    return lax.dot_general(a, b, (dims, ((), ())), preferred_element_type=jnp.float32)


def local(
    sizes,
    block_input,
    cotangent,
    norm1_gain,
    norm1_bias,
    norm2_gain,
    norm2_bias,
    qkv_weight,
    qkv_bias,
    out_weight,
    out_bias,
    up_weight,
    up_bias,
    down_weight,
    down_bias,
    doc_ids,
    doc_start,
):
    fsdp, ctx, count = sizes
    comm = (plain_gather_first, plain_gather_second, plain_scatter_first, plain_scatter_second)
    wide, narrow = jnp.float32, jnp.bfloat16
    own_count, width = block_input.shape
    lw = qkv_weight.shape[2]
    hidden = up_weight.shape[1]
    heads_here = lw // HD
    row_count = own_count * count
    group = fsdp * ctx
    score_scale = HD ** (-0.5)
    piece = qkv_weight.shape[1]
    packed = jnp.concatenate(
        [qkv_weight[0], qkv_weight[1], qkv_weight[2], out_weight.T, up_weight, down_weight.T],
        axis=1,
    )
    packed, full_in = comm[0](packed, block_input, count)
    packed = packed.reshape(width, packed.shape[2])
    full_in = full_in.reshape(row_count, width)
    qkv_full = packed[:, : 3 * lw]
    out_t = packed[:, 3 * lw : 4 * lw]
    up_full = packed[:, 4 * lw : 4 * lw + hidden]
    down_t = packed[:, 4 * lw + hidden :]
    gain_one = norm1_gain.astype(wide)
    gain_two = norm2_gain.astype(wide)
    normed, inv_std = normalize(full_in.astype(wide))
    first_in = (normed * gain_one + norm1_bias.astype(wide)).astype(narrow)
    second_in = (normed * gain_two + norm2_bias.astype(wide)).astype(narrow)
    projected = dot(first_in, qkv_full) + qkv_bias.astype(wide).reshape(1, 3 * lw)
    query_pos = lax.axis_index("ctx") * row_count + jnp.arange(row_count, dtype=jnp.int32)
    cosine, sine_table = angle_tables(query_pos - doc_start)
    queries = rotate(
        projected[:, :lw].reshape(row_count, heads_here, HD), cosine, sine_table
    ).astype(narrow)
    keys_here = rotate(
        projected[:, lw : 2 * lw].reshape(row_count, heads_here, HD), cosine, sine_table
    ).astype(narrow)
    keys_values = jnp.concatenate(
        [keys_here.reshape(row_count, lw), projected[:, 2 * lw :].astype(narrow)], axis=1
    )
    full_cot, keys_values = comm[1](cotangent, keys_values, count)
    full_cot = full_cot.reshape(row_count, width)
    length = ctx * row_count
    keys_values = keys_values.reshape(length, 2 * lw)
    keys_all = keys_values[:, :lw].reshape(length, heads_here, HD)
    values_all = keys_values[:, lw:].reshape(length, heads_here, HD)
    attn_probs = attention_probs(queries, keys_all, query_pos, doc_start)
    probs_b = attn_probs.astype(narrow)
    attended = jnp.einsum("hqk,khd->qhd", probs_b, values_all, preferred_element_type=wide)
    attended = attended.reshape(row_count, lw).astype(narrow)
    pre_act = dot(second_in, up_full) + up_bias.astype(wide)
    activated, gelu_slope = gelu_parts(pre_act)
    act_b = activated.astype(narrow)
    last = ((1,), (1,))
    rows = ((0,), (0,))
    forward = dot(attended, out_t, last) + dot(act_b, down_t, last)
    d_attended = dot(full_cot, out_t).astype(narrow)
    d_pre = (dot(full_cot, down_t) * gelu_slope).astype(narrow)
    grad_up_local = dot(second_in, d_pre, rows)
    grad_down_local = dot(full_cot, act_b, rows)
    up_bias_grad = jnp.sum(d_pre.astype(wide), axis=0)
    d_heads = d_attended.reshape(row_count, heads_here, HD)
    d_values = jnp.einsum("hqk,qhd->khd", probs_b, d_heads, preferred_element_type=wide)
    d_probs = jnp.einsum("qhd,khd->hqk", d_heads, values_all, preferred_element_type=wide)
    delta_sum = jnp.sum(attn_probs * d_probs, axis=2, keepdims=True)
    d_scores = (attn_probs * (d_probs - delta_sum)).astype(narrow)
    d_query = (
        jnp.einsum("hqk,khd->qhd", d_scores, keys_all, preferred_element_type=wide) * score_scale
    )
    d_keys = (
        jnp.einsum("hqk,qhd->khd", d_scores, queries, preferred_element_type=wide) * score_scale
    )
    key_grads = jnp.concatenate([d_keys.reshape(length, lw), d_values.reshape(length, lw)], axis=1)
    key_grads = key_grads.reshape(ctx, row_count, 2 * lw)
    mlp_grads, summed, key_far = comm[2](
        jnp.concatenate([grad_up_local.astype(narrow), grad_down_local.astype(narrow)], axis=1)
        .reshape(group, piece, 2 * hidden),
        forward.astype(narrow).reshape(count, own_count, width),
        key_grads.astype(narrow),
        count,
    )
    block_output = (
        block_input.astype(wide) + summed + out_bias.astype(wide) + down_bias.astype(wide)
    ).astype(narrow)
    key_own = lax.dynamic_index_in_dim(key_grads, lax.axis_index("ctx"), 0, keepdims=False)
    key_own = key_own + key_far.astype(wide)
    d_qkv = jnp.concatenate(
        [
            rotate(d_query, cosine, -sine_table).reshape(row_count, lw),
            rotate(
                key_own[:, :lw].reshape(row_count, heads_here, HD), cosine, -sine_table
            ).reshape(row_count, lw),
            key_own[:, lw:],
        ],
        axis=1,
    ).astype(narrow)
    qkv_bias_grad = jnp.sum(d_qkv.astype(wide), axis=0)
    grad_qkv_local = dot(first_in, d_qkv, rows)
    grad_out_local = dot(full_cot, attended, rows)
    d_first = dot(d_qkv, qkv_full, last)
    d_second = dot(d_pre, up_full, last)
    cot_float = cotangent.astype(wide)
    span = max(width, hidden, 3 * lw)

    def pad(row):
        return jnp.pad(row, (0, span - row.shape[0]))

    small = jnp.stack(
        [
            pad(row)
            for row in (
                jnp.sum(cot_float, axis=0),
                jnp.sum(d_first * normed, axis=0),
                jnp.sum(d_first, axis=0),
                jnp.sum(d_second * normed, axis=0),
                jnp.sum(d_second, axis=0),
                up_bias_grad,
                qkv_bias_grad,
                jnp.zeros((width,), wide),
            )
        ]
    )
    partial = d_first * gain_one + d_second * gain_two
    attn_grads, combined, small = comm[3](
        jnp.concatenate([grad_qkv_local.astype(narrow), grad_out_local.astype(narrow)], axis=1)
        .reshape(group, piece, 4 * lw),
        partial.astype(narrow).reshape(count, own_count, width),
        small,
        count,
        5,
    )
    normed_own, inv_own = normalize(block_input.astype(wide))
    mean_one = jnp.mean(combined, axis=1, keepdims=True)
    mean_two = jnp.mean(combined * normed_own, axis=1, keepdims=True)
    grad_input = (cot_float + inv_own * (combined - mean_one - normed_own * mean_two)).astype(narrow)
    return (
        block_output,
        grad_input,
        attn_grads[:, : 3 * lw].reshape(piece, 3, lw).transpose(1, 0, 2),
        small[6, : 3 * lw].reshape(3, lw),
        attn_grads[:, 3 * lw :].T,
        small[0, :width],
        mlp_grads[:, :hidden],
        small[5, :hidden],
        mlp_grads[:, hidden:].T,
        small[0, :width],
        small[1, :width],
        small[2, :width],
        small[3, :width],
        small[4, :width],
    )


def solution(mesh):
    in_specs = (
        P(("fsdp", "ctx", "tp"), None),
        P(("fsdp", "ctx", "tp"), None),
        P(),
        P(),
        P(),
        P(),
        P(None, ("fsdp", "ctx"), "tp"),
        P(None, "tp"),
        P("tp", ("fsdp", "ctx")),
        P(),
        P(("fsdp", "ctx"), "tp"),
        P("tp"),
        P("tp", ("fsdp", "ctx")),
        P(),
        P(("fsdp", "ctx")),
        P(("fsdp", "ctx")),
    )
    out_specs = (
        P(("fsdp", "ctx", "tp"), None),
        P(("fsdp", "ctx", "tp"), None),
        P(None, ("fsdp", "ctx"), "tp"),
        P(None, "tp"),
        P("tp", ("fsdp", "ctx")),
        P(),
        P(("fsdp", "ctx"), "tp"),
        P("tp"),
        P("tp", ("fsdp", "ctx")),
        P(),
        P(),
        P(),
        P(),
        P(),
    )
    sizes = tuple(mesh.shape[axis] for axis in ("fsdp", "ctx", "tp"))
    fused = sizes[0] == 4 and sizes[1] == 2 and sizes[2] > 1
    body = functools.partial(fused_local if fused else local, sizes)
    return jax.shard_map(body, mesh=mesh, in_specs=in_specs, out_specs=out_specs, check_vma=False)
```

```python
import jax
import jax.numpy as jnp
from jax import lax
from jax.experimental import pallas as pl
from jax.experimental.pallas import tpu as pltpu
import functools
import types
from jax.sharding import PartitionSpec as P

HD = 64
ROT = 16


EPS = 1e-05


def gelu_parts(pre_act):
    cumulative = 0.5 * (1.0 + jax.scipy.special.erf(pre_act * 0.7071067811865476))
    density = jnp.exp(-0.5 * pre_act * pre_act) * 0.3989422804014327
    return (pre_act * cumulative, cumulative + pre_act * density)


def angle_tables(offsets):
    half_rot = ROT // 2
    frequency = 10000.0 ** (-(2.0 * jnp.arange(half_rot, dtype=jnp.float32)) / ROT)
    angles = offsets.astype(jnp.float32)[:, None] * frequency[None, :]
    angles = jnp.concatenate([angles, angles], axis=1)
    return (jnp.cos(angles), jnp.sin(angles))


def rotate(tensor, cosine, sine_table):
    half_rot = ROT // 2
    turned = jnp.concatenate([-tensor[..., half_rot:ROT], tensor[..., :half_rot]], axis=-1)
    leading = tensor[..., :ROT] * cosine[:, None, :] + turned * sine_table[:, None, :]
    return jnp.concatenate([leading, tensor[..., ROT:]], axis=-1)


def normalize(rows_in):
    centered = rows_in - jnp.mean(rows_in, axis=1, keepdims=True)
    inv_std = lax.rsqrt(jnp.mean(centered * centered, axis=1, keepdims=True) + EPS)
    return (centered * inv_std, inv_std)


MESH = pl.DeviceIdType.MESH
VMEM = pl.BlockSpec(memory_space=pltpu.VMEM)
ANY = pl.BlockSpec(memory_space=pl.ANY)
PLANE = ("fsdp", "ctx")


def position():
    f = lax.axis_index("fsdp")
    return lax.rem(f, 2), f // 2, lax.axis_index("ctx"), lax.axis_index("tp")


def partner():
    core, y, _, _ = position()
    return {"fsdp": y * 2 + 1 - core}


def x_peer():
    return {"ctx": 1 - lax.axis_index("ctx")}


def y_peer():
    core, y, _, _ = position()
    return {"fsdp": (1 - y) * 2 + core}


def plane_peer(step):
    rank = lax.rem(lax.axis_index("fsdp") * 2 + lax.axis_index("ctx") + step, 8)
    return {"fsdp": rank // 2, "ctx": lax.rem(rank, 2)}


def z_peer(step, count):
    return {"tp": lax.rem(lax.axis_index("tp") + step, count)}


def greet(peers):
    barrier = pltpu.get_barrier_semaphore()
    for peer in peers:
        pl.semaphore_signal(barrier, inc=1, device_id=peer, device_id_type=MESH)
    pl.semaphore_wait(barrier, len(peers))


def remote(src, dst, sems, k, peer):
    return pltpu.make_async_remote_copy(
        src_ref=src,
        dst_ref=dst,
        send_sem=sems[0].at[k],
        recv_sem=sems[1].at[k],
        device_id=peer,
        device_id_type=MESH,
    )


def run_all(*parts):
    parts = list(parts)
    while parts:
        parts = [part for part in parts if next(part, "end") != "end"]


def plane_scatter(src, out, core_in, summed, side_in, mixed, last_in, sems):
    core, y, x, _ = position()
    half = out.shape[0] // 2
    rows = (pl.ds(0, half), pl.ds(half, half))
    to_p, to_x, to_y = partner(), x_peer(), y_peer()
    wide = jnp.float32
    first = []
    for q in range(4):
        there = ((q // 2) * 2 + 1 - core) * 2 + q % 2
        first.append(remote(src.at[there], core_in.at[q], sems, q, to_p))
    for copy in first:
        copy.start()
    yield
    for q in range(4):
        first[q].wait_recv()
        here = ((q // 2) * 2 + core) * 2 + q % 2
        summed[q] = (src[here].astype(wide) + core_in[q].astype(wide)).astype(summed.dtype)
    second = [
        remote(summed.at[(1 - y) * 2 + 1 - x, rows[0]], side_in.at[0], sems, 4, to_x),
        remote(summed.at[(1 - y) * 2 + 1 - x, rows[1]], side_in.at[1], sems, 5, to_y),
        remote(summed.at[y * 2 + 1 - x, rows[0]], side_in.at[2], sems, 6, to_x),
        remote(summed.at[(1 - y) * 2 + x, rows[1]], side_in.at[3], sems, 7, to_y),
    ]
    for copy in second:
        copy.start()
    yield
    third = []
    for k, (where, peer) in enumerate((((1 - y) * 2 + x, to_y), (y * 2 + 1 - x, to_x))):
        second[k].wait_recv()
        total = summed[where, rows[k]].astype(wide) + side_in[k].astype(wide)
        mixed[k] = total.astype(mixed.dtype)
        copy = remote(mixed.at[k], last_in.at[k], sems, 8 + k, peer)
        copy.start()
        third.append(copy)
    yield
    for k in range(2):
        second[2 + k].wait_recv()
        third[k].wait_recv()
        out[rows[k]] = (
            summed[y * 2 + x, rows[k]].astype(wide)
            + side_in[2 + k].astype(wide)
            + last_in[k].astype(wide)
        )
    for copy in first + second + third:
        copy.wait_send()


def z_scatter(src, out, landed, sems, count):
    t = lax.axis_index("tp")
    copies = []
    for d in range(1, count):
        peer = z_peer(d, count)
        copies.append(remote(src.at[peer["tp"]], landed.at[d - 1], sems, d - 1, peer))
    for copy in copies:
        copy.start()
    yield
    yield
    yield
    total = src[t].astype(jnp.float32)
    for d in range(1, count):
        copies[d - 1].wait()
        total = total + landed[d - 1].astype(jnp.float32)
    out[...] = total


def sem_pair(count):
    return [pltpu.SemaphoreType.DMA((count,)), pltpu.SemaphoreType.DMA((count,))]


def call(body, outs, out_specs, inputs, scratch, collective):
    return pl.pallas_call(
        body,
        out_shape=outs,
        in_specs=[VMEM] * len(inputs),
        out_specs=out_specs,
        scratch_shapes=scratch,
        compiler_params=pltpu.CompilerParams(
            collective_id=collective, has_side_effects=True, vmem_limit_bytes=48 * 1024 * 1024
        ),
    )(*inputs)


def shape(dims, dtype=jnp.bfloat16):
    return jax.ShapeDtypeStruct(dims, dtype)


def ready(generator):
    return next(generator, "end")


def plane_spread(src, out, sems, own_sem, tilt):
    core, y, x, _ = position()
    half = src.shape[0] // 2
    first, second = pl.ds(0, half), pl.ds(half, half)

    def slot(yy, xx):
        return (yy * 2 + core) * 2 + xx

    own, from_x, from_y, diag = slot(y, x), slot(y, 1 - x), slot(1 - y, x), slot(1 - y, 1 - x)
    to_p, to_x, to_y = partner(), x_peer(), y_peer()
    made = {}

    def begin(k, where, rows, peer):
        place = out.at[where, rows]
        made[k] = remote(src.at[rows] if k < 4 else place, place, sems, k, peer)
        made[k].start()

    begin(0, own, first, to_x)
    begin(1, own, second, to_y)
    begin(2, own, second, to_x)
    begin(3, own, first, to_y)
    made[4] = remote(src, out.at[own], sems, 4, to_p)
    keep = pltpu.make_async_copy(src, out.at[own], own_sem)
    made[4].start()
    keep.start()
    yield
    made[0].wait_recv()
    begin(5, from_x, first, to_y)
    begin(7, from_x, first, to_p)
    made[1].wait_recv()
    if not tilt:
        begin(6, from_y, second, to_x)
    begin(8, from_y, second, to_p)
    yield
    made[2].wait_recv()
    if tilt:
        begin(6, from_x, second, to_y)
    begin(9, from_x, second, to_p)
    made[3].wait_recv()
    begin(10, from_y, first, to_p)
    yield
    made[5].wait_recv()
    begin(11, diag, first, to_p)
    made[6].wait_recv()
    begin(12, diag, second, to_p)
    yield
    for k in (4, 7, 8, 9, 10, 11, 12):
        made[k].wait_recv()
    for k in range(13):
        made[k].wait_send()
    keep.wait()


def row_sum(src, out, plane_in, middle, z_in, sems, count, shared):
    t = lax.axis_index("tp")
    rank = lax.axis_index("fsdp") * 2 + lax.axis_index("ctx")
    ones = [
        remote(src.at[lax.rem(rank + d, 8)], plane_in.at[rank], sems[0], d - 1, plane_peer(d))
        for d in range(1, 8)
    ]
    for copy in ones:
        copy.start()
    plane_in[rank] = src[rank]
    yield
    for copy in ones:
        copy.wait()
    total = plane_in[0]
    for i in range(1, 8):
        total = total + plane_in[i]
    middle[0] = total
    twos = [
        remote(middle.at[0], z_in.at[t], sems[1], d - 1, z_peer(d, count)) for d in range(1, count)
    ]
    for copy in twos:
        copy.start()
    z_in[t] = total
    yield
    for copy in twos:
        copy.wait()
    all_sum = z_in[0]
    for i in range(1, count):
        all_sum = all_sum + z_in[i]
    middle[1] = jnp.where(rank < shared, all_sum, middle[0])
    threes = [
        remote(middle.at[1], out.at[rank], sems[2], d - 1, plane_peer(d)) for d in range(1, 8)
    ]
    for copy in threes:
        copy.start()
    out[rank] = middle[1]
    yield
    for copy in threes:
        copy.wait()


def line_gather(arrays, count):
    t = lax.axis_index("tp")
    far_up, far_down = t, count - 1 - t

    def copy(item, upward, j):
        src, out, ups, downs = arrays[item]
        if upward:
            where = out.at[jnp.clip(t - j, 0, count - 1)]
            peer = {"tp": jnp.minimum(t + 1, count - 1)}
        else:
            where = out.at[jnp.clip(t + j, 0, count - 1)]
            peer = {"tp": jnp.maximum(t - 1, 0)}
        sems = ups if upward else downs
        k = jnp.clip(j, 0, count - 2)
        return where, remote(where, where, sems, k, peer), remote(src, where, sems, k, peer)

    for s in range(2 * count):
        for item in range(len(arrays)):
            for upward in (True, False):
                reach = far_up if upward else far_down
                limit = far_down if upward else far_up
                j = s - item * (reach + 1)

                @pl.when((j >= 1) & (j <= reach))
                def _():
                    copy(item, upward, j - 1)[1].wait_recv()

                @pl.when((j == 0) & (limit > 0))
                def _():
                    copy(item, upward, j)[2].start()

                @pl.when((j >= 1) & (j <= reach) & (limit > 0))
                def _():
                    copy(item, upward, j)[1].start()

        yield
    for item in range(len(arrays)):
        for upward in (True, False):
            reach = far_up if upward else far_down
            limit = far_down if upward else far_up
            for j in range(count - 1):

                @pl.when((j <= reach) & (limit > 0))
                def _():
                    copy(item, upward, j)[1].wait_send()


def lanes(dims):
    return lax.broadcasted_iota(jnp.int32, dims, len(dims) - 1)


def rotate_tile(tile, tables, sign):
    turned = pltpu.roll(tile, 128 - ROT // 2, 1) * tables[1] + pltpu.roll(tile, ROT // 2, 1) * tables[2]
    return tile * tables[0] + sign * turned


def fused_kernel(names, count, *refs):
    r = types.SimpleNamespace(**dict(zip(names, refs)))
    wide, narrow = jnp.float32, jnp.bfloat16
    _, _, x, t = position()
    row_count, width = r.normed.shape
    heads_here = r.qs.shape[0]
    own_count = row_count // count
    piece = r.pack_a.shape[0]
    lw = heads_here * HD
    block = min(256, row_count)
    blocks = row_count // block
    last, rows = ((1,), (1,)), ((0,), (0,))
    half_rot = ROT // 2
    params = r.params
    hidden = r.wu.shape[2]
    kv_sem = (r.kv_send, r.kv_recv)
    far_sem = (r.far_send, r.far_recv)

    def span(b):
        return pl.ds(pl.multiple_of(b * block, block), block)

    def each_block(step):
        lax.fori_loop(0, blocks, lambda b, _: (step(b), 0)[1], 0)

    def pair(name):
        return (getattr(r, name + "_s"), getattr(r, name + "_r"))

    def square(ref):
        return ref[...].reshape(ref.shape[0] * ref.shape[1], ref.shape[2])

    loads = [
        pltpu.make_async_copy(a, b, r.load.at[k])
        for k, (a, b) in enumerate(
            (
                (r.qkv, r.raw_qkv),
                (r.outw, r.raw_out),
                (r.qkv_bias, r.raw_bias),
                (r.doc_start, r.raw_start),
                (r.gain_one, r.v_gain_one),
                (r.bias_one, r.v_bias_one),
                (r.gain_two, r.v_gain_two),
                (r.bias_two, r.v_bias_two),
                (r.up_bias, r.v_up_bias),
                (r.out_bias, r.v_out_bias),
                (r.down_bias, r.v_down_bias),
            )
        )
    ]
    for copy in loads:
        copy.start()
    greet([plane_peer(i) for i in range(1, 8)] + [z_peer(i, count) for i in range(1, count)])
    zg = line_gather(
        [
            (r.rows, r.full_in, pair("zru"), pair("zrd")),
            (r.cot, r.full_cot, pair("zcu"), pair("zcd")),
        ],
        count,
    )
    ga = plane_spread(r.pack_a, r.wa, pair("ga"), r.own.at[2], False)
    gu = plane_spread(r.up, r.wu, pair("gu"), r.own.at[3], True)
    gd = plane_spread(r.down, r.wd, pair("gd"), r.own.at[4], True)
    ready(zg)
    keeps = [
        pltpu.make_async_copy(r.rows, r.full_in.at[t], r.own.at[0]),
        pltpu.make_async_copy(r.cot, r.full_cot.at[t], r.own.at[1]),
    ]
    for copy in keeps:
        copy.start()

    def turn_over(value):
        n = value.shape[1]
        one = (lax.broadcasted_iota(jnp.int32, (n, n), 0) == lanes((n, n))).astype(narrow)
        return dot(one, value, last).astype(narrow)

    loads[0].wait()
    loads[1].wait()
    out_t = turn_over(r.raw_out[...])
    tiles = []
    for h in range(heads_here):
        cut = slice(h * HD, (h + 1) * HD)
        tiles += [r.raw_qkv[1][:, cut], r.raw_qkv[2][:, cut]]
    for h in range(heads_here):
        cut = slice(h * HD, (h + 1) * HD)
        tiles += [r.raw_qkv[0][:, cut], out_t[:, cut]]
    r.pack_a[...] = jnp.concatenate(tiles, axis=1)
    ready(ga)
    for copy in loads[2:]:
        copy.wait()

    def row_of(ref):
        return ref[...].astype(wide).reshape(1, ref.shape[0])

    params[...] = jnp.zeros_like(params)
    params[0:1, :width] = row_of(r.v_gain_one)
    params[1:2, :width] = row_of(r.v_bias_one)
    params[2:3, :width] = row_of(r.v_gain_two)
    params[3:4, :width] = row_of(r.v_bias_two)
    bias = r.raw_bias[...].astype(wide)
    tiles = []
    for h in range(heads_here):
        cut = slice(h * HD, (h + 1) * HD)
        tiles += [bias[1:2, cut], bias[2:3, cut]]
    for h in range(heads_here):
        tiles += [bias[0:1, h * HD : (h + 1) * HD], jnp.zeros((1, HD), wide)]
    params[4:5, : 4 * lw] = jnp.concatenate(tiles, axis=1)
    params[5:6, :hidden] = row_of(r.v_up_bias)
    params[6:7, :width] = row_of(r.v_out_bias) + row_of(r.v_down_bias)

    lane = lanes((8, 128))
    sub = lax.broadcasted_iota(jnp.int32, (8, 128), 0)
    is_key = lane < HD
    low = ((lane == sub) & is_key).astype(wide)
    high = ((lane == sub + half_rot) & is_key).astype(wide)

    def expand(value, table):
        return lax.dot_general(
            value, table, (rows, ((), ())), precision=lax.Precision.HIGHEST, preferred_element_type=wide
        )

    start = jnp.broadcast_to(r.raw_start[...].reshape(1, row_count), (half_rot, row_count))
    dims = (half_rot, row_count)
    which = lax.broadcasted_iota(jnp.int32, dims, 0)
    frequency = jnp.zeros(dims, wide)
    for i in range(half_rot):
        frequency = jnp.where(which == i, 10000.0 ** (-2.0 * i / ROT), frequency)
    angles = (x * row_count + lanes(dims) - start).astype(wide) * frequency
    rest = (lanes((1, 128)) >= ROT).astype(wide)
    r.tables[0] = expand(jnp.cos(angles), low + high) + rest
    r.tables[1] = expand(jnp.sin(angles), -low)
    r.tables[2] = expand(jnp.sin(angles), high)
    r.start[...] = expand(start.astype(wide), (sub == 0).astype(wide))
    key_scale = (lanes((1, 128)) < HD).astype(wide) * HD ** (-0.5)
    value_mask = (lanes((1, 128)) >= HD).astype(wide)

    def chunk(c):
        return pl.ds(pl.multiple_of(c * own_count, own_count), own_count)

    def norm_chunk(c):
        values = r.full_in[c].astype(wide)
        normed, inv_std = normalize(values)
        r.normed[chunk(c)] = normed
        r.inv[chunk(c)] = jnp.broadcast_to(inv_std, (own_count, 128))
        r.first[chunk(c)] = (normed * params[0:1, :width] + params[1:2, :width]).astype(narrow)
        r.second[chunk(c)] = (normed * params[2:3, :width] + params[3:4, :width]).astype(narrow)

    def tables_at(where):
        return [r.tables[k, where] for k in range(3)]

    def kv_copy(c):
        place = r.kv.at[:, chunk(c)]
        return remote(place, place, kv_sem, c, x_peer())

    def project(c):
        tabs = tables_at(chunk(c))
        out = dot(r.first[chunk(c)], square(r.wa)) + params[4:5, : 4 * lw]
        where = pl.ds(pl.multiple_of(x * row_count + c * own_count, own_count), own_count)
        for h in range(heads_here):
            tile = out[:, h * 128 : (h + 1) * 128]
            r.kv[h, where] = rotate_tile(tile, tabs, 1.0).astype(narrow)
            tile = out[:, (heads_here + h) * 128 : (heads_here + h + 1) * 128]
            r.qs[h, chunk(c)] = (rotate_tile(tile, tabs, 1.0) * key_scale).astype(narrow)

        @pl.when(x == 0)
        def _():
            kv_copy(c).start()

    def up(c):
        pre = dot(r.second[chunk(c)], square(r.wu)) + params[5:6, :hidden]
        activated, slope = gelu_parts(pre)
        r.act[chunk(c)] = activated.astype(narrow)
        r.slope[chunk(c)] = slope

    def arrived(s, *steps):
        if s == 0:
            for step in steps:
                step(t)
            return

        def side(k, _):
            c = t - s + 2 * s * k

            @pl.when((c >= 0) & (c < count))
            def _():
                for step in steps:
                    step(c)

            return 0

        lax.fori_loop(0, 2, side, 0)

    def down(b):
        r.forward[span(b)] = dot(r.act[span(b)], square(r.wd), last)

    def attend(side, begin, end):
        def head(h, _):
            for b in range(blocks):
                keys = side * row_count + (b + 1) * block
                cut = pl.ds(b * block, block)
                kv = r.kv[h, pl.ds(0, keys)]
                scores = dot(r.qs[h, cut], kv, last)
                key_pos = lanes((block, keys))
                query_pos = side * row_count + b * block + lax.broadcasted_iota(jnp.int32, (block, keys), 0)
                start = r.start[cut, 0:1].astype(jnp.int32)
                allowed = (key_pos >= start) & (key_pos <= query_pos)
                scores = jnp.where(allowed, scores, -1e30)
                exponent = jnp.exp(scores - jnp.max(scores, axis=1, keepdims=True))
                probs = exponent * (1.0 / jnp.sum(exponent, axis=1, keepdims=True))
                r.probs[h, cut, pl.ds(0, keys)] = probs
                r.attz[h, cut] = (dot(probs.astype(narrow), kv) * value_mask).astype(narrow)
            return 0

        lax.fori_loop(begin, end, head, 0)

    def attend_heads(begin, end):
        for side in range(2):
            pl.when(x == side)(functools.partial(attend, side, begin, end))

    def keys_arrive():
        @pl.when(x == 1)
        def _():
            for c in range(count):
                kv_copy(c).wait_recv()

    def heads_of(ref, where):
        return jnp.concatenate([ref[h, where] for h in range(heads_here)], axis=1)

    def chunks(b):
        per = block // own_count
        return pl.ds(b * per, per)

    query_cut = slice(2 * lw, 4 * lw)

    def finish_forward(b):
        weight = square(r.wa)[:, query_cut]
        total = r.forward[span(b)] + dot(heads_of(r.attz, span(b)), weight, last)
        r.fs_src[chunks(b)] = total.astype(narrow).reshape(block // own_count, own_count, width)

    fs = z_scatter(r.fs_src, r.fs_sum, r.fs_land, pair("fs"), count)

    def back(c):
        cot = r.full_cot[c]
        d_att = dot(cot, square(r.wa)[:, query_cut])
        for h in range(heads_here):
            r.az[h, chunk(c)] = (d_att[:, h * 128 : (h + 1) * 128] * value_mask).astype(narrow)
        d_pre = (dot(cot, square(r.wd)) * r.slope[chunk(c)]).astype(narrow)
        r.d_pre[chunk(c)] = d_pre
        r.small_src[5, :, :hidden] += jnp.sum(d_pre.astype(wide), axis=0, keepdims=True)
        d_second = dot(d_pre, square(r.wu), last)
        r.small_src[3, :, :width] += jnp.sum(d_second * r.normed[chunk(c)], axis=0, keepdims=True)
        r.small_src[4, :, :width] += jnp.sum(d_second, axis=0, keepdims=True)
        r.d_second[chunk(c)] = d_second * params[2:3, :width]

    def cot_arrived(*steps):
        def side(k, _):
            for s in steps:
                up_hop, down_hop = s - t - 1, s - count + t
                c = jnp.where(k == 0, t - up_hop, t + down_hop)
                hop = jnp.where(k == 0, up_hop, down_hop)

                @pl.when((hop >= 1) & (c >= 0) & (c < count))
                def _():
                    back(c)

            return 0

        lax.fori_loop(0, 2, side, 0)

    r.small_src[...] = jnp.zeros_like(r.small_src)

    def own_cot():
        return r.full_cot[t].astype(wide)

    ready(gu)
    ready(gd)
    keeps[0].wait()
    arrived(0, norm_chunk)
    ready(ga)
    ready(zg)
    arrived(1, norm_chunk)
    ready(ga)
    ready(gu)
    ready(gd)
    ready(zg)
    arrived(2, norm_chunk)
    ready(ga)
    ready(gu)
    ready(gd)
    ready(zg)
    ready(ga)
    arrived(0, project)
    arrived(1, project)
    arrived(2, project)
    arrived(3, norm_chunk)
    arrived(3, project)
    ready(gu)
    ready(gu)
    arrived(0, up)
    arrived(1, up)
    ready(zg)
    ready(gd)
    ready(gd)
    keeps[1].wait()
    arrived(2, up)
    arrived(3, up)
    each_block(down)
    keys_arrive()
    attend_heads(0, 1)
    ready(zg)
    attend_heads(1, heads_here)
    each_block(finish_forward)
    ready(fs)
    back(t)
    cot_arrived(3)
    cot_arrived(4)
    cot_arrived(5)
    ready(zg)
    cot_arrived(6)
    ready(zg)
    cot_arrived(7)
    ready(zg)

    @pl.when(x == 0)
    def _():
        for c in range(count):
            kv_copy(c).wait_send()

    def far(h):
        return remote(r.far_src.at[h], r.far_in.at[h], far_sem, h, x_peer())

    def attend_back(side):
        def head(h, _):
            for b in reversed(range(blocks)):
                keys = side * row_count + (b + 1) * block
                cut, used = pl.ds(b * block, block), pl.ds(0, keys)
                probs, kv = r.probs[h, cut, used], r.kv[h, used]
                d_att, query = r.az[h, cut], r.qs[h, cut]
                d_probs = dot(d_att, kv, last)
                delta = jnp.sum(probs * d_probs, axis=1, keepdims=True)
                d_scores = (probs * (d_probs - delta)).astype(narrow)
                d_query = rotate_tile(dot(d_scores, kv), [r.tables[k, cut] for k in range(3)], -1.0)
                r.d_query[h, cut] = (d_query * key_scale).astype(narrow)
                grads = dot(d_scores, query, rows) + dot(probs.astype(narrow), d_att, rows)
                if b == blocks - 1:
                    r.d_kv[h, used] = grads
                else:
                    r.d_kv[h, used] += grads
            if side == 1:
                r.far_src[h] = r.d_kv[h, pl.ds(0, row_count)].astype(narrow)
                far(h).start()
            return 0

        lax.fori_loop(0, heads_here, head, 0)

    for side in range(2):
        pl.when(x == side)(functools.partial(attend_back, side))

    cot_all = square(r.full_cot)
    group = r.gu_src.shape[0]

    def to_pieces(value):
        return value.astype(narrow).reshape(group, piece, value.shape[1])

    def scatter(form, name, out):
        parts = [getattr(r, name + k) for k in "abcde"]
        return form(getattr(r, name + "_src"), out, *parts, pair(name + "s"))

    su, sd = scatter(plane_scatter, "gu", r.sum_u), scatter(plane_scatter, "gd", r.sum_d)
    sa = scatter(plane_scatter, "ga", r.sum_a)
    r.gu_src[...] = to_pieces(dot(r.second[...], r.d_pre[...], rows))
    ready(su)
    r.gd_src[...] = to_pieces(dot(cot_all, r.act[...], rows))
    ready(sd)

    ready(su)
    ready(sd)
    for h in range(heads_here):

        @pl.when(x == 0)
        def _():
            far(h).wait_recv()
            r.d_kv[h, pl.ds(0, row_count)] += r.far_in[h].astype(wide)

    def gather_grads(b):
        tabs = tables_at(span(b))
        where = pl.ds(pl.multiple_of(x * row_count + b * block, block), block)
        for h in range(heads_here):
            value = rotate_tile(r.d_kv[h, where], tabs, -1.0).astype(narrow)
            r.d_pack[span(b), h * 128 : (h + 1) * 128] = value
            cut = slice((heads_here + h) * 128, (heads_here + h + 1) * 128)
            r.d_pack[span(b), cut] = r.d_query[h, span(b)]
        d_pack = r.d_pack[span(b)]
        r.small_src[6, :, : 4 * lw] += jnp.sum(d_pack.astype(wide), axis=0, keepdims=True)
        d_first = dot(d_pack, square(r.wa), last)
        r.small_src[1, :, :width] += jnp.sum(d_first * r.normed[span(b)], axis=0, keepdims=True)
        r.small_src[2, :, :width] += jnp.sum(d_first, axis=0, keepdims=True)
        total = d_first * params[0:1, :width] + r.d_second[span(b)]
        r.gs_src[chunks(b)] = total.astype(narrow).reshape(block // own_count, own_count, width)

    r.small_src[0, :, :width] = jnp.sum(own_cot(), axis=0, keepdims=True)
    each_block(gather_grads)
    sm = row_sum(
        r.small_src, r.small_sum, r.small_p, r.small_mid, r.small_z,
        (pair("sma"), pair("smb"), pair("smc")), count, 5,
    )
    ready(sm)
    gs = z_scatter(r.gs_src, r.gs_sum, r.gs_land, pair("gs"), count)
    ready(sm)
    ready(gs)
    ready(su)
    first_all = r.first[...]
    r.ga_src[:, :, : 2 * lw] = to_pieces(dot(first_all, r.d_pack[:, : 2 * lw], rows))
    mixed = dot(first_all, r.d_pack[:, query_cut], rows)
    mixed += dot(cot_all, heads_of(r.attz, slice(None)), rows)
    r.ga_src[:, :, query_cut] = to_pieces(mixed)
    ready(sa)
    ready(sd)
    ready(sm)
    ready(su)
    ready(sa)
    ready(sd)
    for _ in range(3):
        ready(fs)
    base = r.full_in[t].astype(wide) + r.fs_sum[...]
    r.v_rows[...] = (base + params[6:7, :width]).astype(narrow)
    results = [
        pltpu.make_async_copy(a, b, r.store.at[k])
        for k, (a, b) in enumerate(
            (
                (r.v_rows, r.out_rows),
                (r.sum_u, r.out_u),
                (r.sum_d, r.out_d),
                (r.v_qkv, r.out_qkv),
                (r.v_out, r.out_out),
                (r.v_grad, r.out_grad),
                (r.small_sum, r.out_small),
                (r.v_bias, r.out_bias_qkv),
            )
        )
    ]
    for copy in results[:3]:
        copy.start()
    ready(sa)
    ready(sa)

    def split_tiles(value):
        halves = [value[:, k * HD : (k + 1) * HD] for k in range(4 * heads_here)]
        keys, values = halves[0 : 2 * heads_here : 2], halves[1 : 2 * heads_here : 2]
        return [jnp.concatenate(v, axis=1) for v in (halves[2 * heads_here :: 2], keys, values)]

    total = r.sum_a[...]
    for k, value in enumerate(split_tiles(total)):
        r.v_qkv[k] = value
    one = lax.broadcasted_iota(jnp.int32, (piece, piece), 0) == lanes((piece, piece))
    for h in range(heads_here):
        cut = slice((heads_here + h) * 128, (heads_here + h + 1) * 128)
        r.v_out[h * HD : (h + 1) * HD] = expand(total[:, cut], one.astype(wide))[HD:]
    results[3].start()
    results[4].start()
    ready(sm)
    for k, value in enumerate(split_tiles(r.small_sum[6][:, : 4 * lw])):
        r.v_bias[k : k + 1] = value
    results[6].start()
    results[7].start()
    for _ in range(3):
        ready(gs)
    mine = pl.ds(pl.multiple_of(t * own_count, own_count), own_count)
    combined, normed = r.gs_sum[...], r.normed[mine]
    mean_one = jnp.mean(combined, axis=1, keepdims=True)
    mean_two = jnp.mean(combined * normed, axis=1, keepdims=True)
    grad = own_cot() + r.inv[mine, 0:1] * (combined - mean_one - normed * mean_two)
    r.v_grad[...] = grad.astype(narrow)
    results[5].start()

    @pl.when(x == 1)
    def _():
        for h in range(heads_here):
            far(h).wait_send()

    for copy in results:
        copy.wait()
    run_all(zg, ga, gu, gd, su, sd, sa, fs, gs, sm)


def fused_call(arrays, count):
    own, width = arrays["rows"].shape
    piece, hidden = arrays["up"].shape
    lw = arrays["qkv"].shape[2]
    heads = lw // HD
    row_count = own * count
    group = 8
    wide, narrow = jnp.float32, jnp.bfloat16
    pack = 4 * lw
    small = (8, max(width, hidden, pack))
    outs = dict(
        out_rows=((own, width), narrow),
        out_grad=((own, width), narrow),
        out_qkv=((3, piece, lw), wide),
        out_out=((lw, piece), wide),
        out_u=((piece, hidden), wide),
        out_d=((piece, hidden), wide),
        out_small=((8, 1, small[1]), wide),
        out_bias_qkv=((3, lw), wide),
    )
    scratch = dict(
        raw_qkv=(arrays["qkv"].shape, narrow),
        raw_out=(arrays["outw"].shape, narrow),
        raw_bias=((3, lw), narrow),
        raw_start=((row_count,), jnp.int32),
        v_gain_one=((width,), narrow),
        v_bias_one=((width,), narrow),
        v_gain_two=((width,), narrow),
        v_bias_two=((width,), narrow),
        v_up_bias=((hidden,), narrow),
        v_out_bias=((width,), narrow),
        v_down_bias=((width,), narrow),
        params=(small, wide),
        sum_a=((piece, pack), wide),
        sum_u=((piece, hidden), wide),
        sum_d=((piece, hidden), wide),
        small_sum=((8, 1, small[1]), wide),
        v_rows=((own, width), narrow),
        v_grad=((own, width), narrow),
        v_qkv=((3, piece, lw), wide),
        v_out=((lw, piece), wide),
        v_bias=((3, lw), wide),
        pack_a=((piece, pack), narrow),
        wa=((group, piece, pack), narrow),
        wu=((group, piece, hidden), narrow),
        wd=((group, piece, hidden), narrow),
        full_in=((count, own, width), narrow),
        full_cot=((count, own, width), narrow),
        tables=((3, row_count, 128), wide),
        start=((row_count, 128), wide),
        normed=((row_count, width), wide),
        inv=((row_count, 128), wide),
        first=((row_count, width), narrow),
        second=((row_count, width), narrow),
        kv=((heads, 2 * row_count, 128), narrow),
        qs=((heads, row_count, 128), narrow),
        az=((heads, row_count, 128), narrow),
        attz=((heads, row_count, 128), narrow),
        act=((row_count, hidden), narrow),
        slope=((row_count, hidden), wide),
        forward=((row_count, width), wide),
        probs=((heads, row_count, 2 * row_count), wide),
        d_pre=((row_count, hidden), narrow),
        d_second=((row_count, width), wide),
        d_query=((heads, row_count, 128), narrow),
        d_kv=((heads, 2 * row_count, 128), wide),
        far_src=((heads, row_count, 128), narrow),
        far_in=((heads, row_count, 128), narrow),
        d_pack=((row_count, pack), narrow),
        fs_src=((count, own, width), narrow),
        fs_land=((count - 1, own, width), narrow),
        fs_sum=((own, width), wide),
        gs_src=((count, own, width), narrow),
        gs_land=((count - 1, own, width), narrow),
        gs_sum=((own, width), wide),
        small_src=((8, 1, small[1]), wide),
        small_z=((count, 1, small[1]), wide),
        small_mid=((2, 1, small[1]), wide),
        small_p=((group, 1, small[1]), wide),
    )
    half = piece // 2
    for name, span in dict(ga=pack, gu=hidden, gd=hidden).items():
        scratch[name + "_src"] = ((group, piece, span), narrow)
        for k, dims in zip("abcde", ((4, piece), (4, piece), (4, half), (2, half), (2, half))):
            scratch[name + k] = (dims + (span,), narrow)
    sems = dict(load=11, store=8, own=5, kv_send=count, kv_recv=count, far_send=heads, far_recv=heads)
    z = count - 1
    pairs = dict(zru=z, zrd=z, zcu=z, zcd=z, fs=z, gs=z, sma=7, smb=z, smc=7)
    pairs.update(ga=13, gu=13, gd=13, gas=10, gus=10, gds=10)
    for name, number in pairs.items():
        sems[name + "_s"] = sems[name + "_r"] = number
    names = list(arrays) + list(outs) + list(scratch) + list(sems)
    buffers = [pltpu.VMEM(dims, kind) for dims, kind in scratch.values()]
    buffers += [pltpu.SemaphoreType.DMA((number,)) for number in sems.values()]
    return pl.pallas_call(
        functools.partial(fused_kernel, names, count),
        out_shape=[shape(dims, kind) for dims, kind in outs.values()],
        in_specs=[ANY] * len(arrays),
        out_specs=[ANY] * len(outs),
        scratch_shapes=buffers,
        compiler_params=pltpu.CompilerParams(
            collective_id=0, has_side_effects=True, vmem_limit_bytes=60 * 1024 * 1024
        ),
    )(*arrays.values())


def last_call(given, width, hidden):
    def body(*refs):
        small, bias = refs[6], refs[7]
        given, outs, sem = refs[:6], refs[8:22], refs[22]
        places = (0, 1, 2, 4, 6, 8)
        copies = [
            pltpu.make_async_copy(src, outs[k], sem.at[i])
            for i, (src, k) in enumerate(zip(given, places))
        ]
        for copy in copies:
            copy.start()
        outs[3][...] = bias[...]
        for k, row in ((5, 0), (9, 0), (10, 1), (11, 2), (12, 3), (13, 4)):
            outs[k][...] = small[row, 0, :width]
        outs[7][...] = small[5, 0, :hidden]
        for copy in copies:
            copy.wait()

    wide = jnp.float32
    vector = shape((width,), wide)
    shapes = [shape(v.shape, v.dtype) for v in given]
    outs = shapes[:3] + [shapes[7], shapes[3], vector, shapes[4], shape((hidden,), wide), shapes[5]]
    outs += [vector] * 5
    specs = [ANY] * 3 + [VMEM, ANY, VMEM, ANY, VMEM, ANY] + [VMEM] * 5
    return pl.pallas_call(
        body,
        out_shape=outs,
        in_specs=[VMEM] * 8,
        out_specs=specs,
        scratch_shapes=[pltpu.SemaphoreType.DMA((6,))],
        compiler_params=pltpu.CompilerParams(vmem_limit_bytes=60 * 1024 * 1024),
    )(*given)


def fused_local(
    sizes,
    block_input,
    cotangent,
    norm1_gain,
    norm1_bias,
    norm2_gain,
    norm2_bias,
    qkv_weight,
    qkv_bias,
    out_weight,
    out_bias,
    up_weight,
    up_bias,
    down_weight,
    down_bias,
    doc_ids,
    doc_start,
):
    count = sizes[2]
    arrays = dict(rows=block_input, cot=cotangent, up=up_weight, qkv=qkv_weight, outw=out_weight)
    arrays.update(down=down_weight.T, gain_one=norm1_gain, bias_one=norm1_bias)
    arrays.update(gain_two=norm2_gain, bias_two=norm2_bias, up_bias=up_bias, out_bias=out_bias)
    arrays.update(down_bias=down_bias, qkv_bias=qkv_bias, doc_start=doc_start)
    out = list(last_call(fused_call(arrays, count), block_input.shape[1], up_bias.shape[0]))
    out[8] = out[8].T
    return tuple(out)


def plain_gather_first(weights, rows, count):
    return lax.all_gather(weights, PLANE), lax.all_gather(rows, "tp")


def plain_gather_second(rows, keys, count):
    return lax.all_gather(rows, "tp"), lax.all_gather(keys, "ctx")


def plain_scatter(grads, partial):
    grads = lax.psum_scatter(grads.astype(jnp.float32), PLANE, scatter_dimension=0)
    return grads, lax.psum_scatter(partial.astype(jnp.float32), "tp", scatter_dimension=0)


def plain_scatter_first(grads, partial, key_grads, count):
    x = lax.axis_index("ctx")
    total = lax.psum_scatter(key_grads.astype(jnp.float32), "ctx", scatter_dimension=0)
    own = lax.dynamic_index_in_dim(key_grads, x, 0, keepdims=False)
    return plain_scatter(grads, partial) + (total - own.astype(jnp.float32),)


def plain_scatter_second(grads, partial, small, count, shared):
    total = lax.psum(small, PLANE)
    return plain_scatter(grads, partial) + (
        jnp.concatenate([lax.psum(total[:shared], "tp"), total[shared:]]),
    )


def attention_probs(queries, keys_all, query_pos, query_start):
    score_scale = HD ** (-0.5)
    scores = (
        jnp.einsum("qhd,khd->hqk", queries, keys_all, preferred_element_type=jnp.float32)
        * score_scale
    )
    key_pos = jnp.arange(keys_all.shape[0], dtype=jnp.int32)
    allowed = (key_pos[None, :] >= query_start[:, None]) & (key_pos[None, :] <= query_pos[:, None])
    masked = jnp.where(allowed[None], scores, -1e30)
    row_peak = jnp.max(masked, axis=2, keepdims=True)
    exponent = jnp.where(allowed[None], jnp.exp(masked - row_peak), 0.0)
    return exponent / jnp.sum(exponent, axis=2, keepdims=True)


def dot(a, b, dims=((1,), (0,))):
    return lax.dot_general(a, b, (dims, ((), ())), preferred_element_type=jnp.float32)


def local(
    sizes,
    block_input,
    cotangent,
    norm1_gain,
    norm1_bias,
    norm2_gain,
    norm2_bias,
    qkv_weight,
    qkv_bias,
    out_weight,
    out_bias,
    up_weight,
    up_bias,
    down_weight,
    down_bias,
    doc_ids,
    doc_start,
):
    fsdp, ctx, count = sizes
    comm = (plain_gather_first, plain_gather_second, plain_scatter_first, plain_scatter_second)
    wide, narrow = jnp.float32, jnp.bfloat16
    own_count, width = block_input.shape
    lw = qkv_weight.shape[2]
    hidden = up_weight.shape[1]
    heads_here = lw // HD
    row_count = own_count * count
    group = fsdp * ctx
    score_scale = HD ** (-0.5)
    piece = qkv_weight.shape[1]
    packed = jnp.concatenate(
        [qkv_weight[0], qkv_weight[1], qkv_weight[2], out_weight.T, up_weight, down_weight.T],
        axis=1,
    )
    packed, full_in = comm[0](packed, block_input, count)
    packed = packed.reshape(width, packed.shape[2])
    full_in = full_in.reshape(row_count, width)
    qkv_full = packed[:, : 3 * lw]
    out_t = packed[:, 3 * lw : 4 * lw]
    up_full = packed[:, 4 * lw : 4 * lw + hidden]
    down_t = packed[:, 4 * lw + hidden :]
    gain_one = norm1_gain.astype(wide)
    gain_two = norm2_gain.astype(wide)
    normed, inv_std = normalize(full_in.astype(wide))
    first_in = (normed * gain_one + norm1_bias.astype(wide)).astype(narrow)
    second_in = (normed * gain_two + norm2_bias.astype(wide)).astype(narrow)
    projected = dot(first_in, qkv_full) + qkv_bias.astype(wide).reshape(1, 3 * lw)
    query_pos = lax.axis_index("ctx") * row_count + jnp.arange(row_count, dtype=jnp.int32)
    cosine, sine_table = angle_tables(query_pos - doc_start)
    queries = rotate(
        projected[:, :lw].reshape(row_count, heads_here, HD), cosine, sine_table
    ).astype(narrow)
    keys_here = rotate(
        projected[:, lw : 2 * lw].reshape(row_count, heads_here, HD), cosine, sine_table
    ).astype(narrow)
    keys_values = jnp.concatenate(
        [keys_here.reshape(row_count, lw), projected[:, 2 * lw :].astype(narrow)], axis=1
    )
    full_cot, keys_values = comm[1](cotangent, keys_values, count)
    full_cot = full_cot.reshape(row_count, width)
    length = ctx * row_count
    keys_values = keys_values.reshape(length, 2 * lw)
    keys_all = keys_values[:, :lw].reshape(length, heads_here, HD)
    values_all = keys_values[:, lw:].reshape(length, heads_here, HD)
    attn_probs = attention_probs(queries, keys_all, query_pos, doc_start)
    probs_b = attn_probs.astype(narrow)
    attended = jnp.einsum("hqk,khd->qhd", probs_b, values_all, preferred_element_type=wide)
    attended = attended.reshape(row_count, lw).astype(narrow)
    pre_act = dot(second_in, up_full) + up_bias.astype(wide)
    activated, gelu_slope = gelu_parts(pre_act)
    act_b = activated.astype(narrow)
    last = ((1,), (1,))
    rows = ((0,), (0,))
    forward = dot(attended, out_t, last) + dot(act_b, down_t, last)
    d_attended = dot(full_cot, out_t).astype(narrow)
    d_pre = (dot(full_cot, down_t) * gelu_slope).astype(narrow)
    grad_up_local = dot(second_in, d_pre, rows)
    grad_down_local = dot(full_cot, act_b, rows)
    up_bias_grad = jnp.sum(d_pre.astype(wide), axis=0)
    d_heads = d_attended.reshape(row_count, heads_here, HD)
    d_values = jnp.einsum("hqk,qhd->khd", probs_b, d_heads, preferred_element_type=wide)
    d_probs = jnp.einsum("qhd,khd->hqk", d_heads, values_all, preferred_element_type=wide)
    delta_sum = jnp.sum(attn_probs * d_probs, axis=2, keepdims=True)
    d_scores = (attn_probs * (d_probs - delta_sum)).astype(narrow)
    d_query = (
        jnp.einsum("hqk,khd->qhd", d_scores, keys_all, preferred_element_type=wide) * score_scale
    )
    d_keys = (
        jnp.einsum("hqk,qhd->khd", d_scores, queries, preferred_element_type=wide) * score_scale
    )
    key_grads = jnp.concatenate([d_keys.reshape(length, lw), d_values.reshape(length, lw)], axis=1)
    key_grads = key_grads.reshape(ctx, row_count, 2 * lw)
    mlp_grads, summed, key_far = comm[2](
        jnp.concatenate([grad_up_local.astype(narrow), grad_down_local.astype(narrow)], axis=1)
        .reshape(group, piece, 2 * hidden),
        forward.astype(narrow).reshape(count, own_count, width),
        key_grads.astype(narrow),
        count,
    )
    block_output = (
        block_input.astype(wide) + summed + out_bias.astype(wide) + down_bias.astype(wide)
    ).astype(narrow)
    key_own = lax.dynamic_index_in_dim(key_grads, lax.axis_index("ctx"), 0, keepdims=False)
    key_own = key_own + key_far.astype(wide)
    d_qkv = jnp.concatenate(
        [
            rotate(d_query, cosine, -sine_table).reshape(row_count, lw),
            rotate(
                key_own[:, :lw].reshape(row_count, heads_here, HD), cosine, -sine_table
            ).reshape(row_count, lw),
            key_own[:, lw:],
        ],
        axis=1,
    ).astype(narrow)
    qkv_bias_grad = jnp.sum(d_qkv.astype(wide), axis=0)
    grad_qkv_local = dot(first_in, d_qkv, rows)
    grad_out_local = dot(full_cot, attended, rows)
    d_first = dot(d_qkv, qkv_full, last)
    d_second = dot(d_pre, up_full, last)
    cot_float = cotangent.astype(wide)
    span = max(width, hidden, 3 * lw)

    def pad(row):
        return jnp.pad(row, (0, span - row.shape[0]))

    small = jnp.stack(
        [
            pad(row)
            for row in (
                jnp.sum(cot_float, axis=0),
                jnp.sum(d_first * normed, axis=0),
                jnp.sum(d_first, axis=0),
                jnp.sum(d_second * normed, axis=0),
                jnp.sum(d_second, axis=0),
                up_bias_grad,
                qkv_bias_grad,
                jnp.zeros((width,), wide),
            )
        ]
    )
    partial = d_first * gain_one + d_second * gain_two
    attn_grads, combined, small = comm[3](
        jnp.concatenate([grad_qkv_local.astype(narrow), grad_out_local.astype(narrow)], axis=1)
        .reshape(group, piece, 4 * lw),
        partial.astype(narrow).reshape(count, own_count, width),
        small,
        count,
        5,
    )
    normed_own, inv_own = normalize(block_input.astype(wide))
    mean_one = jnp.mean(combined, axis=1, keepdims=True)
    mean_two = jnp.mean(combined * normed_own, axis=1, keepdims=True)
    grad_input = (cot_float + inv_own * (combined - mean_one - normed_own * mean_two)).astype(narrow)
    return (
        block_output,
        grad_input,
        attn_grads[:, : 3 * lw].reshape(piece, 3, lw).transpose(1, 0, 2),
        small[6, : 3 * lw].reshape(3, lw),
        attn_grads[:, 3 * lw :].T,
        small[0, :width],
        mlp_grads[:, :hidden],
        small[5, :hidden],
        mlp_grads[:, hidden:].T,
        small[0, :width],
        small[1, :width],
        small[2, :width],
        small[3, :width],
        small[4, :width],
    )


def solution(mesh):
    in_specs = (
        P(("fsdp", "ctx", "tp"), None),
        P(("fsdp", "ctx", "tp"), None),
        P(),
        P(),
        P(),
        P(),
        P(None, ("fsdp", "ctx"), "tp"),
        P(None, "tp"),
        P("tp", ("fsdp", "ctx")),
        P(),
        P(("fsdp", "ctx"), "tp"),
        P("tp"),
        P("tp", ("fsdp", "ctx")),
        P(),
        P(("fsdp", "ctx")),
        P(("fsdp", "ctx")),
    )
    out_specs = (
        P(("fsdp", "ctx", "tp"), None),
        P(("fsdp", "ctx", "tp"), None),
        P(None, ("fsdp", "ctx"), "tp"),
        P(None, "tp"),
        P("tp", ("fsdp", "ctx")),
        P(),
        P(("fsdp", "ctx"), "tp"),
        P("tp"),
        P("tp", ("fsdp", "ctx")),
        P(),
        P(),
        P(),
        P(),
        P(),
    )
    sizes = tuple(mesh.shape[axis] for axis in ("fsdp", "ctx", "tp"))
    fused = sizes[0] == 4 and sizes[1] == 2 and sizes[2] == 4
    body = functools.partial(fused_local if fused else local, sizes)
    return jax.shard_map(body, mesh=mesh, in_specs=in_specs, out_specs=out_specs, check_vma=False)
```

```python
import jax
import jax.numpy as jnp
from jax import lax
from jax.experimental import pallas as pl
from jax.experimental.pallas import tpu as pltpu
import functools
import types
from jax.sharding import PartitionSpec as P

HD = 64
ROT = 16


EPS = 1e-05


def gelu_parts(pre_act):
    cumulative = 0.5 * (1.0 + jax.scipy.special.erf(pre_act * 0.7071067811865476))
    density = jnp.exp(-0.5 * pre_act * pre_act) * 0.3989422804014327
    return (pre_act * cumulative, cumulative + pre_act * density)


def angle_tables(offsets):
    half_rot = ROT // 2
    frequency = 10000.0 ** (-(2.0 * jnp.arange(half_rot, dtype=jnp.float32)) / ROT)
    angles = offsets.astype(jnp.float32)[:, None] * frequency[None, :]
    angles = jnp.concatenate([angles, angles], axis=1)
    return (jnp.cos(angles), jnp.sin(angles))


def rotate(tensor, cosine, sine_table):
    half_rot = ROT // 2
    turned = jnp.concatenate([-tensor[..., half_rot:ROT], tensor[..., :half_rot]], axis=-1)
    leading = tensor[..., :ROT] * cosine[:, None, :] + turned * sine_table[:, None, :]
    return jnp.concatenate([leading, tensor[..., ROT:]], axis=-1)


def normalize(rows_in):
    centered = rows_in - jnp.mean(rows_in, axis=1, keepdims=True)
    inv_std = lax.rsqrt(jnp.mean(centered * centered, axis=1, keepdims=True) + EPS)
    return (centered * inv_std, inv_std)


MESH = pl.DeviceIdType.MESH
VMEM = pl.BlockSpec(memory_space=pltpu.VMEM)
ANY = pl.BlockSpec(memory_space=pl.ANY)
PLANE = ("fsdp", "ctx")


def position():
    f = lax.axis_index("fsdp")
    return lax.rem(f, 2), f // 2, lax.axis_index("ctx"), lax.axis_index("tp")


def partner():
    core, y, _, _ = position()
    return {"fsdp": y * 2 + 1 - core}


def x_peer():
    return {"ctx": 1 - lax.axis_index("ctx")}


def y_peer():
    core, y, _, _ = position()
    return {"fsdp": (1 - y) * 2 + core}


def plane_peer(step):
    rank = lax.rem(lax.axis_index("fsdp") * 2 + lax.axis_index("ctx") + step, 8)
    return {"fsdp": rank // 2, "ctx": lax.rem(rank, 2)}


def z_peer(step, count):
    return {"tp": lax.rem(lax.axis_index("tp") + step, count)}


def greet(peers):
    barrier = pltpu.get_barrier_semaphore()
    for peer in peers:
        pl.semaphore_signal(barrier, inc=1, device_id=peer, device_id_type=MESH)
    pl.semaphore_wait(barrier, len(peers))


def remote(src, dst, sems, k, peer):
    return pltpu.make_async_remote_copy(
        src_ref=src,
        dst_ref=dst,
        send_sem=sems[0].at[k],
        recv_sem=sems[1].at[k],
        device_id=peer,
        device_id_type=MESH,
    )


def run_all(*parts):
    parts = list(parts)
    while parts:
        parts = [part for part in parts if next(part, "end") != "end"]


def plane_scatter(src, out, core_in, summed, side_in, mixed, last_in, sems):
    core, y, x, _ = position()
    half = out.shape[0] // 2
    rows = (pl.ds(0, half), pl.ds(half, half))
    to_p, to_x, to_y = partner(), x_peer(), y_peer()
    wide = jnp.float32
    first = []
    for q in range(4):
        there = ((q // 2) * 2 + 1 - core) * 2 + q % 2
        first.append(remote(src.at[there], core_in.at[q], sems, q, to_p))
    for copy in first:
        copy.start()
    yield
    for q in range(4):
        first[q].wait_recv()
        here = ((q // 2) * 2 + core) * 2 + q % 2
        summed[q] = (src[here].astype(wide) + core_in[q].astype(wide)).astype(summed.dtype)
    second = [
        remote(summed.at[(1 - y) * 2 + 1 - x, rows[0]], side_in.at[0], sems, 4, to_x),
        remote(summed.at[(1 - y) * 2 + 1 - x, rows[1]], side_in.at[1], sems, 5, to_y),
        remote(summed.at[y * 2 + 1 - x, rows[0]], side_in.at[2], sems, 6, to_x),
        remote(summed.at[(1 - y) * 2 + x, rows[1]], side_in.at[3], sems, 7, to_y),
    ]
    for copy in second:
        copy.start()
    yield
    third = []
    for k, (where, peer) in enumerate((((1 - y) * 2 + x, to_y), (y * 2 + 1 - x, to_x))):
        second[k].wait_recv()
        total = summed[where, rows[k]].astype(wide) + side_in[k].astype(wide)
        mixed[k] = total.astype(mixed.dtype)
        copy = remote(mixed.at[k], last_in.at[k], sems, 8 + k, peer)
        copy.start()
        third.append(copy)
    yield
    for k in range(2):
        second[2 + k].wait_recv()
        third[k].wait_recv()
        out[rows[k]] = (
            summed[y * 2 + x, rows[k]].astype(wide)
            + side_in[2 + k].astype(wide)
            + last_in[k].astype(wide)
        )
    for copy in first + second + third:
        copy.wait_send()


def z_scatter(src, out, landed, sems, count):
    t = lax.axis_index("tp")
    copies = []
    for d in range(1, count):
        peer = z_peer(d, count)
        copies.append(remote(src.at[peer["tp"]], landed.at[d - 1], sems, d - 1, peer))
    for copy in copies:
        copy.start()
    yield
    yield
    yield
    total = src[t].astype(jnp.float32)
    for d in range(1, count):
        copies[d - 1].wait()
        total = total + landed[d - 1].astype(jnp.float32)
    out[...] = total


def sem_pair(count):
    return [pltpu.SemaphoreType.DMA((count,)), pltpu.SemaphoreType.DMA((count,))]


def call(body, outs, out_specs, inputs, scratch, collective):
    return pl.pallas_call(
        body,
        out_shape=outs,
        in_specs=[VMEM] * len(inputs),
        out_specs=out_specs,
        scratch_shapes=scratch,
        compiler_params=pltpu.CompilerParams(
            collective_id=collective, has_side_effects=True, vmem_limit_bytes=48 * 1024 * 1024
        ),
    )(*inputs)


def shape(dims, dtype=jnp.bfloat16):
    return jax.ShapeDtypeStruct(dims, dtype)


def ready(generator):
    return next(generator, "end")


def plane_spread(src, out, sems, own_sem, tilt):
    core, y, x, _ = position()
    half = src.shape[0] // 2
    first, second = pl.ds(0, half), pl.ds(half, half)

    def slot(yy, xx):
        return (yy * 2 + core) * 2 + xx

    own, from_x, from_y, diag = slot(y, x), slot(y, 1 - x), slot(1 - y, x), slot(1 - y, 1 - x)
    to_p, to_x, to_y = partner(), x_peer(), y_peer()
    made = {}

    def begin(k, where, rows, peer):
        place = out.at[where, rows]
        made[k] = remote(src.at[rows] if k < 4 else place, place, sems, k, peer)
        made[k].start()

    begin(0, own, first, to_x)
    begin(1, own, second, to_y)
    begin(2, own, second, to_x)
    begin(3, own, first, to_y)
    made[4] = remote(src, out.at[own], sems, 4, to_p)
    keep = pltpu.make_async_copy(src, out.at[own], own_sem)
    made[4].start()
    keep.start()
    yield
    made[0].wait_recv()
    begin(5, from_x, first, to_y)
    begin(7, from_x, first, to_p)
    made[1].wait_recv()
    if not tilt:
        begin(6, from_y, second, to_x)
    begin(8, from_y, second, to_p)
    yield
    made[2].wait_recv()
    if tilt:
        begin(6, from_x, second, to_y)
    begin(9, from_x, second, to_p)
    made[3].wait_recv()
    begin(10, from_y, first, to_p)
    yield
    made[5].wait_recv()
    begin(11, diag, first, to_p)
    made[6].wait_recv()
    begin(12, diag, second, to_p)
    yield
    for k in (4, 7, 8, 9, 10, 11, 12):
        made[k].wait_recv()
    for k in range(13):
        made[k].wait_send()
    keep.wait()


def row_sum(src, out, plane_in, middle, z_in, sems, count, shared):
    t = lax.axis_index("tp")
    rank = lax.axis_index("fsdp") * 2 + lax.axis_index("ctx")
    ones = [
        remote(src.at[lax.rem(rank + d, 8)], plane_in.at[rank], sems[0], d - 1, plane_peer(d))
        for d in range(1, 8)
    ]
    for copy in ones:
        copy.start()
    plane_in[rank] = src[rank]
    yield
    for copy in ones:
        copy.wait()
    total = plane_in[0]
    for i in range(1, 8):
        total = total + plane_in[i]
    middle[0] = total
    twos = [
        remote(middle.at[0], z_in.at[t], sems[1], d - 1, z_peer(d, count)) for d in range(1, count)
    ]
    for copy in twos:
        copy.start()
    z_in[t] = total
    yield
    for copy in twos:
        copy.wait()
    all_sum = z_in[0]
    for i in range(1, count):
        all_sum = all_sum + z_in[i]
    middle[1] = jnp.where(rank < shared, all_sum, middle[0])
    threes = [
        remote(middle.at[1], out.at[rank], sems[2], d - 1, plane_peer(d)) for d in range(1, 8)
    ]
    for copy in threes:
        copy.start()
    out[rank] = middle[1]
    yield
    for copy in threes:
        copy.wait()


def line_gather(arrays, count):
    t = lax.axis_index("tp")
    far_up, far_down = t, count - 1 - t

    def copy(item, upward, j):
        src, out, ups, downs = arrays[item]
        if upward:
            where = out.at[jnp.clip(t - j, 0, count - 1)]
            peer = {"tp": jnp.minimum(t + 1, count - 1)}
        else:
            where = out.at[jnp.clip(t + j, 0, count - 1)]
            peer = {"tp": jnp.maximum(t - 1, 0)}
        sems = ups if upward else downs
        k = jnp.clip(j, 0, count - 2)
        return where, remote(where, where, sems, k, peer), remote(src, where, sems, k, peer)

    for s in range(2 * count):
        for item in range(len(arrays)):
            for upward in (True, False):
                reach = far_up if upward else far_down
                limit = far_down if upward else far_up
                j = s - item * (reach + 1)

                @pl.when((j >= 1) & (j <= reach))
                def _():
                    copy(item, upward, j - 1)[1].wait_recv()

                @pl.when((j == 0) & (limit > 0))
                def _():
                    copy(item, upward, j)[2].start()

                @pl.when((j >= 1) & (j <= reach) & (limit > 0))
                def _():
                    copy(item, upward, j)[1].start()

        yield
    for item in range(len(arrays)):
        for upward in (True, False):
            reach = far_up if upward else far_down
            limit = far_down if upward else far_up
            for j in range(count - 1):

                @pl.when((j <= reach) & (limit > 0))
                def _():
                    copy(item, upward, j)[1].wait_send()


def lanes(dims):
    return lax.broadcasted_iota(jnp.int32, dims, len(dims) - 1)


def rotate_tile(tile, tables, sign):
    turned = pltpu.roll(tile, 128 - ROT // 2, 1) * tables[1] + pltpu.roll(tile, ROT // 2, 1) * tables[2]
    return tile * tables[0] + sign * turned


def fused_kernel(names, count, *refs):
    r = types.SimpleNamespace(**dict(zip(names, refs)))
    wide, narrow = jnp.float32, jnp.bfloat16
    _, _, x, t = position()
    row_count, width = r.normed.shape
    heads_here = r.qs.shape[0]
    own_count = row_count // count
    piece = r.pack_a.shape[0]
    lw = heads_here * HD
    block = min(256, row_count)
    blocks = row_count // block
    last, rows = ((1,), (1,)), ((0,), (0,))
    half_rot = ROT // 2
    params = r.params
    hidden = r.wu.shape[2]
    kv_sem = (r.kv_send, r.kv_recv)
    far_sem = (r.far_send, r.far_recv)

    def span(b):
        return pl.ds(pl.multiple_of(b * block, block), block)

    def each_block(step):
        lax.fori_loop(0, blocks, lambda b, _: (step(b), 0)[1], 0)

    def pair(name):
        return (getattr(r, name + "_s"), getattr(r, name + "_r"))

    def square(ref):
        return ref[...].reshape(ref.shape[0] * ref.shape[1], ref.shape[2])

    loads = [
        pltpu.make_async_copy(a, b, r.load.at[k])
        for k, (a, b) in enumerate(
            (
                (r.qkv, r.raw_qkv),
                (r.outw, r.raw_out),
                (r.qkv_bias, r.raw_bias),
                (r.doc_start, r.raw_start),
                (r.gain_one, r.v_gain_one),
                (r.bias_one, r.v_bias_one),
                (r.gain_two, r.v_gain_two),
                (r.bias_two, r.v_bias_two),
                (r.up_bias, r.v_up_bias),
                (r.out_bias, r.v_out_bias),
                (r.down_bias, r.v_down_bias),
            )
        )
    ]
    for copy in loads:
        copy.start()
    greet([plane_peer(i) for i in range(1, 8)] + [z_peer(i, count) for i in range(1, count)])
    zg = line_gather(
        [
            (r.rows, r.full_in, pair("zru"), pair("zrd")),
            (r.cot, r.full_cot, pair("zcu"), pair("zcd")),
        ],
        count,
    )
    ga = plane_spread(r.pack_a, r.wa, pair("ga"), r.own.at[2], False)
    gu = plane_spread(r.up, r.wu, pair("gu"), r.own.at[3], True)
    gd = plane_spread(r.down, r.wd, pair("gd"), r.own.at[4], True)
    ready(zg)
    keeps = [
        pltpu.make_async_copy(r.rows, r.full_in.at[t], r.own.at[0]),
        pltpu.make_async_copy(r.cot, r.full_cot.at[t], r.own.at[1]),
    ]
    for copy in keeps:
        copy.start()

    def turn_over(value):
        n = value.shape[1]
        one = (lax.broadcasted_iota(jnp.int32, (n, n), 0) == lanes((n, n))).astype(narrow)
        return dot(one, value, last).astype(narrow)

    loads[0].wait()
    loads[1].wait()
    out_t = turn_over(r.raw_out[...])
    tiles = []
    for h in range(heads_here):
        cut = slice(h * HD, (h + 1) * HD)
        tiles += [r.raw_qkv[1][:, cut], r.raw_qkv[2][:, cut]]
    for h in range(heads_here):
        cut = slice(h * HD, (h + 1) * HD)
        tiles += [r.raw_qkv[0][:, cut], out_t[:, cut]]
    r.pack_a[...] = jnp.concatenate(tiles, axis=1)
    ready(ga)
    for copy in loads[2:]:
        copy.wait()

    def row_of(ref):
        return ref[...].astype(wide).reshape(1, ref.shape[0])

    params[...] = jnp.zeros_like(params)
    params[0:1, :width] = row_of(r.v_gain_one)
    params[1:2, :width] = row_of(r.v_bias_one)
    params[2:3, :width] = row_of(r.v_gain_two)
    params[3:4, :width] = row_of(r.v_bias_two)
    bias = r.raw_bias[...].astype(wide)
    tiles = []
    for h in range(heads_here):
        cut = slice(h * HD, (h + 1) * HD)
        tiles += [bias[1:2, cut], bias[2:3, cut]]
    for h in range(heads_here):
        tiles += [bias[0:1, h * HD : (h + 1) * HD], jnp.zeros((1, HD), wide)]
    params[4:5, : 4 * lw] = jnp.concatenate(tiles, axis=1)
    params[5:6, :hidden] = row_of(r.v_up_bias)
    params[6:7, :width] = row_of(r.v_out_bias) + row_of(r.v_down_bias)

    lane = lanes((8, 128))
    sub = lax.broadcasted_iota(jnp.int32, (8, 128), 0)
    is_key = lane < HD
    low = ((lane == sub) & is_key).astype(wide)
    high = ((lane == sub + half_rot) & is_key).astype(wide)

    def expand(value, table):
        return lax.dot_general(
            value, table, (rows, ((), ())), precision=lax.Precision.HIGHEST, preferred_element_type=wide
        )

    start = jnp.broadcast_to(r.raw_start[...].reshape(1, row_count), (half_rot, row_count))
    dims = (half_rot, row_count)
    which = lax.broadcasted_iota(jnp.int32, dims, 0)
    frequency = jnp.zeros(dims, wide)
    for i in range(half_rot):
        frequency = jnp.where(which == i, 10000.0 ** (-2.0 * i / ROT), frequency)
    angles = (x * row_count + lanes(dims) - start).astype(wide) * frequency
    rest = (lanes((1, 128)) >= ROT).astype(wide)
    r.tables[0] = expand(jnp.cos(angles), low + high) + rest
    r.tables[1] = expand(jnp.sin(angles), -low)
    r.tables[2] = expand(jnp.sin(angles), high)
    r.start[...] = expand(start.astype(wide), (sub == 0).astype(wide))
    key_scale = (lanes((1, 128)) < HD).astype(wide) * HD ** (-0.5)
    value_mask = (lanes((1, 128)) >= HD).astype(wide)

    def chunk(c):
        return pl.ds(pl.multiple_of(c * own_count, own_count), own_count)

    def norm_chunk(c):
        values = r.full_in[c].astype(wide)
        normed, inv_std = normalize(values)
        r.normed[chunk(c)] = normed
        r.inv[chunk(c)] = jnp.broadcast_to(inv_std, (own_count, 128))
        r.first[chunk(c)] = (normed * params[0:1, :width] + params[1:2, :width]).astype(narrow)
        r.second[chunk(c)] = (normed * params[2:3, :width] + params[3:4, :width]).astype(narrow)

    def tables_at(where):
        return [r.tables[k, where] for k in range(3)]

    def kv_copy(c):
        place = r.kv.at[:, chunk(c)]
        return remote(place, place, kv_sem, c, x_peer())

    def project(c):
        tabs = tables_at(chunk(c))
        out = dot(r.first[chunk(c)], square(r.wa)) + params[4:5, : 4 * lw]
        where = pl.ds(pl.multiple_of(x * row_count + c * own_count, own_count), own_count)
        for h in range(heads_here):
            tile = out[:, h * 128 : (h + 1) * 128]
            r.kv[h, where] = rotate_tile(tile, tabs, 1.0).astype(narrow)
            tile = out[:, (heads_here + h) * 128 : (heads_here + h + 1) * 128]
            r.qs[h, chunk(c)] = (rotate_tile(tile, tabs, 1.0) * key_scale).astype(narrow)

        @pl.when(x == 0)
        def _():
            kv_copy(c).start()

    def up(c):
        pre = dot(r.second[chunk(c)], square(r.wu)) + params[5:6, :hidden]
        activated, slope = gelu_parts(pre)
        r.act[chunk(c)] = activated.astype(narrow)
        r.slope[chunk(c)] = slope

    def arrived(s, *steps):
        if s == 0:
            for step in steps:
                step(t)
            return

        def side(k, _):
            c = t - s + 2 * s * k

            @pl.when((c >= 0) & (c < count))
            def _():
                for step in steps:
                    step(c)

            return 0

        lax.fori_loop(0, 2, side, 0)

    def down(b):
        r.forward[span(b)] = dot(r.act[span(b)], square(r.wd), last)

    def attend(side, begin, end):
        def head(h, _):
            for b in range(blocks):
                keys = side * row_count + (b + 1) * block
                cut = pl.ds(b * block, block)
                kv = r.kv[h, pl.ds(0, keys)]
                scores = dot(r.qs[h, cut], kv, last)
                key_pos = lanes((block, keys))
                query_pos = side * row_count + b * block + lax.broadcasted_iota(jnp.int32, (block, keys), 0)
                start = r.start[cut, 0:1].astype(jnp.int32)
                allowed = (key_pos >= start) & (key_pos <= query_pos)
                scores = jnp.where(allowed, scores, -1e30)
                exponent = jnp.exp(scores - jnp.max(scores, axis=1, keepdims=True))
                probs = exponent * (1.0 / jnp.sum(exponent, axis=1, keepdims=True))
                r.probs[h, cut, pl.ds(0, keys)] = probs
                r.attz[h, cut] = (dot(probs.astype(narrow), kv) * value_mask).astype(narrow)
            return 0

        lax.fori_loop(begin, end, head, 0)

    def attend_heads(begin, end):
        for side in range(2):
            pl.when(x == side)(functools.partial(attend, side, begin, end))

    def keys_arrive():
        @pl.when(x == 1)
        def _():
            for c in range(count):
                kv_copy(c).wait_recv()

    def heads_of(ref, where):
        return jnp.concatenate([ref[h, where] for h in range(heads_here)], axis=1)

    def chunks(b):
        per = block // own_count
        return pl.ds(b * per, per)

    query_cut = slice(2 * lw, 4 * lw)

    def finish_forward(b):
        weight = square(r.wa)[:, query_cut]
        total = r.forward[span(b)] + dot(heads_of(r.attz, span(b)), weight, last)
        r.fs_src[chunks(b)] = total.astype(narrow).reshape(block // own_count, own_count, width)

    fs = z_scatter(r.fs_src, r.fs_sum, r.fs_land, pair("fs"), count)

    def back(c):
        cot = r.full_cot[c]
        d_att = dot(cot, square(r.wa)[:, query_cut])
        for h in range(heads_here):
            r.az[h, chunk(c)] = (d_att[:, h * 128 : (h + 1) * 128] * value_mask).astype(narrow)
        d_pre = (dot(cot, square(r.wd)) * r.slope[chunk(c)]).astype(narrow)
        r.d_pre[chunk(c)] = d_pre
        r.small_src[5, :, :hidden] += jnp.sum(d_pre.astype(wide), axis=0, keepdims=True)

    def cot_arrived(*steps):
        def side(k, _):
            for s in steps:
                up_hop, down_hop = s - t - 1, s - count + t
                c = jnp.where(k == 0, t - up_hop, t + down_hop)
                hop = jnp.where(k == 0, up_hop, down_hop)

                @pl.when((hop >= 1) & (c >= 0) & (c < count))
                def _():
                    back(c)

            return 0

        lax.fori_loop(0, 2, side, 0)

    r.small_src[...] = jnp.zeros_like(r.small_src)

    def own_cot():
        return r.full_cot[t].astype(wide)

    ready(gu)
    ready(gd)
    keeps[0].wait()
    arrived(0, norm_chunk)
    ready(ga)
    ready(zg)
    arrived(1, norm_chunk)
    ready(ga)
    ready(gu)
    ready(gd)
    ready(zg)
    arrived(2, norm_chunk)
    ready(ga)
    ready(gu)
    ready(gd)
    ready(zg)
    ready(ga)
    arrived(0, project)
    arrived(1, project)
    arrived(2, project)
    arrived(3, norm_chunk)
    arrived(3, project)
    ready(gu)
    ready(gu)
    arrived(0, up)
    arrived(1, up)
    ready(zg)
    ready(gd)
    ready(gd)
    keeps[1].wait()
    arrived(2, up)
    arrived(3, up)
    each_block(down)
    keys_arrive()
    attend_heads(0, 1)
    ready(zg)
    attend_heads(1, heads_here)
    each_block(finish_forward)
    ready(fs)
    back(t)
    cot_arrived(3)
    cot_arrived(4)
    cot_arrived(5)
    ready(zg)
    cot_arrived(6)
    ready(zg)
    cot_arrived(7)
    ready(zg)

    @pl.when(x == 0)
    def _():
        for c in range(count):
            kv_copy(c).wait_send()

    def far(h):
        return remote(r.far_src.at[h], r.far_in.at[h], far_sem, h, x_peer())

    def attend_back(side):
        def head(h, _):
            for b in reversed(range(blocks)):
                keys = side * row_count + (b + 1) * block
                cut, used = pl.ds(b * block, block), pl.ds(0, keys)
                probs, kv = r.probs[h, cut, used], r.kv[h, used]
                d_att, query = r.az[h, cut], r.qs[h, cut]
                d_probs = dot(d_att, kv, last)
                delta = jnp.sum(probs * d_probs, axis=1, keepdims=True)
                d_scores = (probs * (d_probs - delta)).astype(narrow)
                d_query = rotate_tile(dot(d_scores, kv), [r.tables[k, cut] for k in range(3)], -1.0)
                r.d_query[h, cut] = (d_query * key_scale).astype(narrow)
                grads = dot(d_scores, query, rows) + dot(probs.astype(narrow), d_att, rows)
                if b == blocks - 1:
                    r.d_kv[h, used] = grads
                else:
                    r.d_kv[h, used] += grads
            if side == 1:
                r.far_src[h] = r.d_kv[h, pl.ds(0, row_count)].astype(narrow)
                far(h).start()
            return 0

        lax.fori_loop(0, heads_here, head, 0)

    for side in range(2):
        pl.when(x == side)(functools.partial(attend_back, side))

    cot_all = square(r.full_cot)
    group = r.gu_src.shape[0]

    def to_pieces(value):
        return value.astype(narrow).reshape(group, piece, value.shape[1])

    def scatter(form, name, out):
        parts = [getattr(r, name + k) for k in "abcde"]
        return form(getattr(r, name + "_src"), out, *parts, pair(name + "s"))

    su, sd = scatter(plane_scatter, "gu", r.sum_u), scatter(plane_scatter, "gd", r.sum_d)
    sa = scatter(plane_scatter, "ga", r.sum_a)
    r.gu_src[...] = to_pieces(dot(r.second[...], r.d_pre[...], rows))
    ready(su)
    r.gd_src[...] = to_pieces(dot(cot_all, r.act[...], rows))
    ready(sd)

    ready(su)
    ready(sd)
    key_cut = slice(0, 2 * lw)

    def second_back(b):
        d_second = dot(r.d_pre[span(b)], square(r.wu), last)
        r.small_src[3, :, :width] += jnp.sum(d_second * r.normed[span(b)], axis=0, keepdims=True)
        r.small_src[4, :, :width] += jnp.sum(d_second, axis=0, keepdims=True)
        r.d_second[span(b)] = d_second * params[2:3, :width]
        d_query = heads_of(r.d_query, span(b))
        r.d_pack[span(b), query_cut] = d_query
        r.small_src[6, :, query_cut] += jnp.sum(d_query.astype(wide), axis=0, keepdims=True)
        r.forward[span(b)] = dot(d_query, square(r.wa)[:, query_cut], last)

    each_block(second_back)
    first_all = r.first[...]
    mixed = dot(first_all, r.d_pack[:, query_cut], rows)
    mixed += dot(cot_all, heads_of(r.attz, slice(None)), rows)
    r.ga_src[:, :, query_cut] = to_pieces(mixed)
    for h in range(heads_here):

        @pl.when(x == 0)
        def _():
            far(h).wait_recv()
            r.d_kv[h, pl.ds(0, row_count)] += r.far_in[h].astype(wide)

    def gather_grads(b):
        tabs = tables_at(span(b))
        where = pl.ds(pl.multiple_of(x * row_count + b * block, block), block)
        for h in range(heads_here):
            value = rotate_tile(r.d_kv[h, where], tabs, -1.0).astype(narrow)
            r.d_pack[span(b), h * 128 : (h + 1) * 128] = value
        d_pack = r.d_pack[span(b), key_cut]
        r.small_src[6, :, key_cut] += jnp.sum(d_pack.astype(wide), axis=0, keepdims=True)
        d_first = r.forward[span(b)] + dot(d_pack, square(r.wa)[:, key_cut], last)
        r.small_src[1, :, :width] += jnp.sum(d_first * r.normed[span(b)], axis=0, keepdims=True)
        r.small_src[2, :, :width] += jnp.sum(d_first, axis=0, keepdims=True)
        total = d_first * params[0:1, :width] + r.d_second[span(b)]
        r.gs_src[chunks(b)] = total.astype(narrow).reshape(block // own_count, own_count, width)

    r.small_src[0, :, :width] = jnp.sum(own_cot(), axis=0, keepdims=True)
    each_block(gather_grads)
    sm = row_sum(
        r.small_src, r.small_sum, r.small_p, r.small_mid, r.small_z,
        (pair("sma"), pair("smb"), pair("smc")), count, 5,
    )
    ready(sm)
    gs = z_scatter(r.gs_src, r.gs_sum, r.gs_land, pair("gs"), count)
    ready(sm)
    ready(gs)
    ready(su)
    r.ga_src[:, :, key_cut] = to_pieces(dot(r.first[...], r.d_pack[:, key_cut], rows))
    ready(sa)
    ready(sd)
    ready(sm)
    ready(su)
    ready(sa)
    ready(sd)
    for _ in range(3):
        ready(fs)
    base = r.full_in[t].astype(wide) + r.fs_sum[...]
    r.v_rows[...] = (base + params[6:7, :width]).astype(narrow)
    results = [
        pltpu.make_async_copy(a, b, r.store.at[k])
        for k, (a, b) in enumerate(
            (
                (r.v_rows, r.out_rows),
                (r.sum_u, r.out_u),
                (r.sum_d, r.out_d),
                (r.v_qkv, r.out_qkv),
                (r.v_out, r.out_out),
                (r.v_grad, r.out_grad),
                (r.small_sum, r.out_small),
                (r.v_bias, r.out_bias_qkv),
            )
        )
    ]
    for copy in results[:3]:
        copy.start()
    ready(sa)
    ready(sa)

    def split_tiles(value):
        halves = [value[:, k * HD : (k + 1) * HD] for k in range(4 * heads_here)]
        keys, values = halves[0 : 2 * heads_here : 2], halves[1 : 2 * heads_here : 2]
        return [jnp.concatenate(v, axis=1) for v in (halves[2 * heads_here :: 2], keys, values)]

    total = r.sum_a[...]
    for k, value in enumerate(split_tiles(total)):
        r.v_qkv[k] = value
    one = lax.broadcasted_iota(jnp.int32, (piece, piece), 0) == lanes((piece, piece))
    for h in range(heads_here):
        cut = slice((heads_here + h) * 128, (heads_here + h + 1) * 128)
        r.v_out[h * HD : (h + 1) * HD] = expand(total[:, cut], one.astype(wide))[HD:]
    results[3].start()
    results[4].start()
    ready(sm)
    for k, value in enumerate(split_tiles(r.small_sum[6][:, : 4 * lw])):
        r.v_bias[k : k + 1] = value
    results[6].start()
    results[7].start()
    for _ in range(3):
        ready(gs)
    mine = pl.ds(pl.multiple_of(t * own_count, own_count), own_count)
    combined, normed = r.gs_sum[...], r.normed[mine]
    mean_one = jnp.mean(combined, axis=1, keepdims=True)
    mean_two = jnp.mean(combined * normed, axis=1, keepdims=True)
    grad = own_cot() + r.inv[mine, 0:1] * (combined - mean_one - normed * mean_two)
    r.v_grad[...] = grad.astype(narrow)
    results[5].start()

    @pl.when(x == 1)
    def _():
        for h in range(heads_here):
            far(h).wait_send()

    for copy in results:
        copy.wait()
    run_all(zg, ga, gu, gd, su, sd, sa, fs, gs, sm)


def fused_call(arrays, count):
    own, width = arrays["rows"].shape
    piece, hidden = arrays["up"].shape
    lw = arrays["qkv"].shape[2]
    heads = lw // HD
    row_count = own * count
    group = 8
    wide, narrow = jnp.float32, jnp.bfloat16
    pack = 4 * lw
    small = (8, max(width, hidden, pack))
    outs = dict(
        out_rows=((own, width), narrow),
        out_grad=((own, width), narrow),
        out_qkv=((3, piece, lw), wide),
        out_out=((lw, piece), wide),
        out_u=((piece, hidden), wide),
        out_d=((piece, hidden), wide),
        out_small=((8, 1, small[1]), wide),
        out_bias_qkv=((3, lw), wide),
    )
    scratch = dict(
        raw_qkv=(arrays["qkv"].shape, narrow),
        raw_out=(arrays["outw"].shape, narrow),
        raw_bias=((3, lw), narrow),
        raw_start=((row_count,), jnp.int32),
        v_gain_one=((width,), narrow),
        v_bias_one=((width,), narrow),
        v_gain_two=((width,), narrow),
        v_bias_two=((width,), narrow),
        v_up_bias=((hidden,), narrow),
        v_out_bias=((width,), narrow),
        v_down_bias=((width,), narrow),
        params=(small, wide),
        sum_a=((piece, pack), wide),
        sum_u=((piece, hidden), wide),
        sum_d=((piece, hidden), wide),
        small_sum=((8, 1, small[1]), wide),
        v_rows=((own, width), narrow),
        v_grad=((own, width), narrow),
        v_qkv=((3, piece, lw), wide),
        v_out=((lw, piece), wide),
        v_bias=((3, lw), wide),
        pack_a=((piece, pack), narrow),
        wa=((group, piece, pack), narrow),
        wu=((group, piece, hidden), narrow),
        wd=((group, piece, hidden), narrow),
        full_in=((count, own, width), narrow),
        full_cot=((count, own, width), narrow),
        tables=((3, row_count, 128), wide),
        start=((row_count, 128), wide),
        normed=((row_count, width), wide),
        inv=((row_count, 128), wide),
        first=((row_count, width), narrow),
        second=((row_count, width), narrow),
        kv=((heads, 2 * row_count, 128), narrow),
        qs=((heads, row_count, 128), narrow),
        az=((heads, row_count, 128), narrow),
        attz=((heads, row_count, 128), narrow),
        act=((row_count, hidden), narrow),
        slope=((row_count, hidden), wide),
        forward=((row_count, width), wide),
        probs=((heads, row_count, 2 * row_count), wide),
        d_pre=((row_count, hidden), narrow),
        d_second=((row_count, width), wide),
        d_query=((heads, row_count, 128), narrow),
        d_kv=((heads, 2 * row_count, 128), wide),
        far_src=((heads, row_count, 128), narrow),
        far_in=((heads, row_count, 128), narrow),
        d_pack=((row_count, pack), narrow),
        fs_src=((count, own, width), narrow),
        fs_land=((count - 1, own, width), narrow),
        fs_sum=((own, width), wide),
        gs_src=((count, own, width), narrow),
        gs_land=((count - 1, own, width), narrow),
        gs_sum=((own, width), wide),
        small_src=((8, 1, small[1]), wide),
        small_z=((count, 1, small[1]), wide),
        small_mid=((2, 1, small[1]), wide),
        small_p=((group, 1, small[1]), wide),
    )
    half = piece // 2
    for name, span in dict(ga=pack, gu=hidden, gd=hidden).items():
        scratch[name + "_src"] = ((group, piece, span), narrow)
        for k, dims in zip("abcde", ((4, piece), (4, piece), (4, half), (2, half), (2, half))):
            scratch[name + k] = (dims + (span,), narrow)
    sems = dict(load=11, store=8, own=5, kv_send=count, kv_recv=count, far_send=heads, far_recv=heads)
    z = count - 1
    pairs = dict(zru=z, zrd=z, zcu=z, zcd=z, fs=z, gs=z, sma=7, smb=z, smc=7)
    pairs.update(ga=13, gu=13, gd=13, gas=10, gus=10, gds=10)
    for name, number in pairs.items():
        sems[name + "_s"] = sems[name + "_r"] = number
    names = list(arrays) + list(outs) + list(scratch) + list(sems)
    buffers = [pltpu.VMEM(dims, kind) for dims, kind in scratch.values()]
    buffers += [pltpu.SemaphoreType.DMA((number,)) for number in sems.values()]
    return pl.pallas_call(
        functools.partial(fused_kernel, names, count),
        out_shape=[shape(dims, kind) for dims, kind in outs.values()],
        in_specs=[ANY] * len(arrays),
        out_specs=[ANY] * len(outs),
        scratch_shapes=buffers,
        compiler_params=pltpu.CompilerParams(
            collective_id=0, has_side_effects=True, vmem_limit_bytes=60 * 1024 * 1024
        ),
    )(*arrays.values())


def last_call(given, width, hidden):
    count = len(given)
    lengths = (width,) * 5 + (hidden,)
    places = (0, 1, 2, 4, 6, 8, None, 3)
    vectors = ((0, 5), (0, 9), (1, 10), (2, 11), (3, 12), (4, 13), (5, 7))

    def body(*refs):
        given, outs, refs = refs[:count], refs[count : count + 14], refs[count + 14 :]
        held, rows, sem, out_sem = refs[:count], refs[count : count + 6], refs[-2], refs[-1]
        loads = [pltpu.make_async_copy(given[k], held[k], sem.at[k]) for k in range(count)]
        for copy in loads:
            copy.start()
        stores = []
        for k, place in enumerate(places):
            if place is not None:
                loads[k].wait()
                stores.append(pltpu.make_async_copy(held[k], outs[place], out_sem.at[len(stores)]))
                stores[-1].start()
        loads[6].wait()
        for k, length in enumerate(lengths):
            rows[k][...] = held[6][k, 0, :length]
        for k, place in vectors:
            stores.append(pltpu.make_async_copy(rows[k], outs[place], out_sem.at[len(stores)]))
            stores[-1].start()
        for copy in stores:
            copy.wait()

    wide = jnp.float32
    vector = shape((width,), wide)
    shapes = [shape(v.shape, v.dtype) for v in given]
    outs = shapes[:3] + [shapes[7], shapes[3], vector, shapes[4], shape((hidden,), wide), shapes[5]]
    outs += [vector] * 5
    scratch = [pltpu.VMEM(v.shape, v.dtype) for v in given]
    scratch += [pltpu.VMEM((length,), wide) for length in lengths]
    return pl.pallas_call(
        body,
        out_shape=outs,
        in_specs=[ANY] * count,
        out_specs=[ANY] * len(outs),
        scratch_shapes=scratch
        + [pltpu.SemaphoreType.DMA((count,)), pltpu.SemaphoreType.DMA((len(outs),))],
        compiler_params=pltpu.CompilerParams(vmem_limit_bytes=60 * 1024 * 1024),
    )(*given)


def fused_local(
    sizes,
    block_input,
    cotangent,
    norm1_gain,
    norm1_bias,
    norm2_gain,
    norm2_bias,
    qkv_weight,
    qkv_bias,
    out_weight,
    out_bias,
    up_weight,
    up_bias,
    down_weight,
    down_bias,
    doc_ids,
    doc_start,
):
    count = sizes[2]
    arrays = dict(rows=block_input, cot=cotangent, up=up_weight, qkv=qkv_weight, outw=out_weight)
    arrays.update(down=down_weight.T, gain_one=norm1_gain, bias_one=norm1_bias)
    arrays.update(gain_two=norm2_gain, bias_two=norm2_bias, up_bias=up_bias, out_bias=out_bias)
    arrays.update(down_bias=down_bias, qkv_bias=qkv_bias, doc_start=doc_start)
    out = list(last_call(fused_call(arrays, count), block_input.shape[1], up_bias.shape[0]))
    out[8] = out[8].T
    return tuple(out)


def plain_gather_first(weights, rows, count):
    return lax.all_gather(weights, PLANE), lax.all_gather(rows, "tp")


def plain_gather_second(rows, keys, count):
    return lax.all_gather(rows, "tp"), lax.all_gather(keys, "ctx")


def plain_scatter(grads, partial):
    grads = lax.psum_scatter(grads.astype(jnp.float32), PLANE, scatter_dimension=0)
    return grads, lax.psum_scatter(partial.astype(jnp.float32), "tp", scatter_dimension=0)


def plain_scatter_first(grads, partial, key_grads, count):
    x = lax.axis_index("ctx")
    total = lax.psum_scatter(key_grads.astype(jnp.float32), "ctx", scatter_dimension=0)
    own = lax.dynamic_index_in_dim(key_grads, x, 0, keepdims=False)
    return plain_scatter(grads, partial) + (total - own.astype(jnp.float32),)


def plain_scatter_second(grads, partial, small, count, shared):
    total = lax.psum(small, PLANE)
    return plain_scatter(grads, partial) + (
        jnp.concatenate([lax.psum(total[:shared], "tp"), total[shared:]]),
    )


def attention_probs(queries, keys_all, query_pos, query_start):
    score_scale = HD ** (-0.5)
    scores = (
        jnp.einsum("qhd,khd->hqk", queries, keys_all, preferred_element_type=jnp.float32)
        * score_scale
    )
    key_pos = jnp.arange(keys_all.shape[0], dtype=jnp.int32)
    allowed = (key_pos[None, :] >= query_start[:, None]) & (key_pos[None, :] <= query_pos[:, None])
    masked = jnp.where(allowed[None], scores, -1e30)
    row_peak = jnp.max(masked, axis=2, keepdims=True)
    exponent = jnp.where(allowed[None], jnp.exp(masked - row_peak), 0.0)
    return exponent / jnp.sum(exponent, axis=2, keepdims=True)


def dot(a, b, dims=((1,), (0,))):
    return lax.dot_general(a, b, (dims, ((), ())), preferred_element_type=jnp.float32)


def local(
    sizes,
    block_input,
    cotangent,
    norm1_gain,
    norm1_bias,
    norm2_gain,
    norm2_bias,
    qkv_weight,
    qkv_bias,
    out_weight,
    out_bias,
    up_weight,
    up_bias,
    down_weight,
    down_bias,
    doc_ids,
    doc_start,
):
    fsdp, ctx, count = sizes
    comm = (plain_gather_first, plain_gather_second, plain_scatter_first, plain_scatter_second)
    wide, narrow = jnp.float32, jnp.bfloat16
    own_count, width = block_input.shape
    lw = qkv_weight.shape[2]
    hidden = up_weight.shape[1]
    heads_here = lw // HD
    row_count = own_count * count
    group = fsdp * ctx
    score_scale = HD ** (-0.5)
    piece = qkv_weight.shape[1]
    packed = jnp.concatenate(
        [qkv_weight[0], qkv_weight[1], qkv_weight[2], out_weight.T, up_weight, down_weight.T],
        axis=1,
    )
    packed, full_in = comm[0](packed, block_input, count)
    packed = packed.reshape(width, packed.shape[2])
    full_in = full_in.reshape(row_count, width)
    qkv_full = packed[:, : 3 * lw]
    out_t = packed[:, 3 * lw : 4 * lw]
    up_full = packed[:, 4 * lw : 4 * lw + hidden]
    down_t = packed[:, 4 * lw + hidden :]
    gain_one = norm1_gain.astype(wide)
    gain_two = norm2_gain.astype(wide)
    normed, inv_std = normalize(full_in.astype(wide))
    first_in = (normed * gain_one + norm1_bias.astype(wide)).astype(narrow)
    second_in = (normed * gain_two + norm2_bias.astype(wide)).astype(narrow)
    projected = dot(first_in, qkv_full) + qkv_bias.astype(wide).reshape(1, 3 * lw)
    query_pos = lax.axis_index("ctx") * row_count + jnp.arange(row_count, dtype=jnp.int32)
    cosine, sine_table = angle_tables(query_pos - doc_start)
    queries = rotate(
        projected[:, :lw].reshape(row_count, heads_here, HD), cosine, sine_table
    ).astype(narrow)
    keys_here = rotate(
        projected[:, lw : 2 * lw].reshape(row_count, heads_here, HD), cosine, sine_table
    ).astype(narrow)
    keys_values = jnp.concatenate(
        [keys_here.reshape(row_count, lw), projected[:, 2 * lw :].astype(narrow)], axis=1
    )
    full_cot, keys_values = comm[1](cotangent, keys_values, count)
    full_cot = full_cot.reshape(row_count, width)
    length = ctx * row_count
    keys_values = keys_values.reshape(length, 2 * lw)
    keys_all = keys_values[:, :lw].reshape(length, heads_here, HD)
    values_all = keys_values[:, lw:].reshape(length, heads_here, HD)
    attn_probs = attention_probs(queries, keys_all, query_pos, doc_start)
    probs_b = attn_probs.astype(narrow)
    attended = jnp.einsum("hqk,khd->qhd", probs_b, values_all, preferred_element_type=wide)
    attended = attended.reshape(row_count, lw).astype(narrow)
    pre_act = dot(second_in, up_full) + up_bias.astype(wide)
    activated, gelu_slope = gelu_parts(pre_act)
    act_b = activated.astype(narrow)
    last = ((1,), (1,))
    rows = ((0,), (0,))
    forward = dot(attended, out_t, last) + dot(act_b, down_t, last)
    d_attended = dot(full_cot, out_t).astype(narrow)
    d_pre = (dot(full_cot, down_t) * gelu_slope).astype(narrow)
    grad_up_local = dot(second_in, d_pre, rows)
    grad_down_local = dot(full_cot, act_b, rows)
    up_bias_grad = jnp.sum(d_pre.astype(wide), axis=0)
    d_heads = d_attended.reshape(row_count, heads_here, HD)
    d_values = jnp.einsum("hqk,qhd->khd", probs_b, d_heads, preferred_element_type=wide)
    d_probs = jnp.einsum("qhd,khd->hqk", d_heads, values_all, preferred_element_type=wide)
    delta_sum = jnp.sum(attn_probs * d_probs, axis=2, keepdims=True)
    d_scores = (attn_probs * (d_probs - delta_sum)).astype(narrow)
    d_query = (
        jnp.einsum("hqk,khd->qhd", d_scores, keys_all, preferred_element_type=wide) * score_scale
    )
    d_keys = (
        jnp.einsum("hqk,qhd->khd", d_scores, queries, preferred_element_type=wide) * score_scale
    )
    key_grads = jnp.concatenate([d_keys.reshape(length, lw), d_values.reshape(length, lw)], axis=1)
    key_grads = key_grads.reshape(ctx, row_count, 2 * lw)
    mlp_grads, summed, key_far = comm[2](
        jnp.concatenate([grad_up_local.astype(narrow), grad_down_local.astype(narrow)], axis=1)
        .reshape(group, piece, 2 * hidden),
        forward.astype(narrow).reshape(count, own_count, width),
        key_grads.astype(narrow),
        count,
    )
    block_output = (
        block_input.astype(wide) + summed + out_bias.astype(wide) + down_bias.astype(wide)
    ).astype(narrow)
    key_own = lax.dynamic_index_in_dim(key_grads, lax.axis_index("ctx"), 0, keepdims=False)
    key_own = key_own + key_far.astype(wide)
    d_qkv = jnp.concatenate(
        [
            rotate(d_query, cosine, -sine_table).reshape(row_count, lw),
            rotate(
                key_own[:, :lw].reshape(row_count, heads_here, HD), cosine, -sine_table
            ).reshape(row_count, lw),
            key_own[:, lw:],
        ],
        axis=1,
    ).astype(narrow)
    qkv_bias_grad = jnp.sum(d_qkv.astype(wide), axis=0)
    grad_qkv_local = dot(first_in, d_qkv, rows)
    grad_out_local = dot(full_cot, attended, rows)
    d_first = dot(d_qkv, qkv_full, last)
    d_second = dot(d_pre, up_full, last)
    cot_float = cotangent.astype(wide)
    span = max(width, hidden, 3 * lw)

    def pad(row):
        return jnp.pad(row, (0, span - row.shape[0]))

    small = jnp.stack(
        [
            pad(row)
            for row in (
                jnp.sum(cot_float, axis=0),
                jnp.sum(d_first * normed, axis=0),
                jnp.sum(d_first, axis=0),
                jnp.sum(d_second * normed, axis=0),
                jnp.sum(d_second, axis=0),
                up_bias_grad,
                qkv_bias_grad,
                jnp.zeros((width,), wide),
            )
        ]
    )
    partial = d_first * gain_one + d_second * gain_two
    attn_grads, combined, small = comm[3](
        jnp.concatenate([grad_qkv_local.astype(narrow), grad_out_local.astype(narrow)], axis=1)
        .reshape(group, piece, 4 * lw),
        partial.astype(narrow).reshape(count, own_count, width),
        small,
        count,
        5,
    )
    normed_own, inv_own = normalize(block_input.astype(wide))
    mean_one = jnp.mean(combined, axis=1, keepdims=True)
    mean_two = jnp.mean(combined * normed_own, axis=1, keepdims=True)
    grad_input = (cot_float + inv_own * (combined - mean_one - normed_own * mean_two)).astype(narrow)
    return (
        block_output,
        grad_input,
        attn_grads[:, : 3 * lw].reshape(piece, 3, lw).transpose(1, 0, 2),
        small[6, : 3 * lw].reshape(3, lw),
        attn_grads[:, 3 * lw :].T,
        small[0, :width],
        mlp_grads[:, :hidden],
        small[5, :hidden],
        mlp_grads[:, hidden:].T,
        small[0, :width],
        small[1, :width],
        small[2, :width],
        small[3, :width],
        small[4, :width],
    )


def solution(mesh):
    in_specs = (
        P(("fsdp", "ctx", "tp"), None),
        P(("fsdp", "ctx", "tp"), None),
        P(),
        P(),
        P(),
        P(),
        P(None, ("fsdp", "ctx"), "tp"),
        P(None, "tp"),
        P("tp", ("fsdp", "ctx")),
        P(),
        P(("fsdp", "ctx"), "tp"),
        P("tp"),
        P("tp", ("fsdp", "ctx")),
        P(),
        P(("fsdp", "ctx")),
        P(("fsdp", "ctx")),
    )
    out_specs = (
        P(("fsdp", "ctx", "tp"), None),
        P(("fsdp", "ctx", "tp"), None),
        P(None, ("fsdp", "ctx"), "tp"),
        P(None, "tp"),
        P("tp", ("fsdp", "ctx")),
        P(),
        P(("fsdp", "ctx"), "tp"),
        P("tp"),
        P("tp", ("fsdp", "ctx")),
        P(),
        P(),
        P(),
        P(),
        P(),
    )
    sizes = tuple(mesh.shape[axis] for axis in ("fsdp", "ctx", "tp"))
    fused = sizes[0] == 4 and sizes[1] == 2 and sizes[2] == 4
    body = functools.partial(fused_local if fused else local, sizes)
    return jax.shard_map(body, mesh=mesh, in_specs=in_specs, out_specs=out_specs, check_vma=False)
```
